512 devices in a mesh: row: 32 (over z_hi, y, core), col: 16 (over z_lo, x).
Axes of the slice: x: 4, y: 8, z: 8 (z_hi: 2, z_lo: 4; z = z_hi * 4 + z_lo), core: 2. Of those that a mesh axis runs over, the one named last changes fastest.
Arguments:
- mask_logits: float32 [4096, 2048], P('row', 'col'), may hold values from -6 to 6
- target: float32 [4096, 2048], P('row', 'col'), may hold values from 0 to 1
- weight: float32 [4096, 2048], P('row', 'col'), may hold values from 0.004 to 10, as said below
- kernels: float32 [2, 12288], P(None, ('row', 'col')), may hold values from -3 to 3
Outputs:
- new_logits: float32 [4096, 2048], P('row', 'col')
- loss_value: float32 [], replicated
The draws below stay inside these ranges and needn't reach their ends.
Inputs may be any that keep to these rules, and one draw needn't show every extreme that they name: `weight`: positive loss weights.
All inputs are finite; a program needn't handle non-finite values.
Results may differ from the reference program's by a relative error of at most 0.0003.
Values sent between devices are 32-bit elements; how exact they have to be, the bound alone decides.
A program may use at most 64 MiB of HBM per device.

```python
import math
import jax
import jax.numpy as jnp
from jax import lax

PAD = 256
HALO = 64
KERNELS = 6
BAND = 32
CONDITIONS = 2
CORE = 128
ROWS = 4096
COLUMNS = 2048
BANK_SIZE = 12288


def draw_weight(key, part):
    key_rows, key_cols, key_cells = jax.random.split(key, 3)
    row_ramp = jnp.exp(math.log(3.0) * jnp.arange(ROWS, dtype=jnp.float32) / ROWS)
    col_ramp = jnp.exp(math.log(3.0) * jnp.arange(COLUMNS, dtype=jnp.float32) / COLUMNS)
    spread = math.log(3.5)
    floor_value = 0.5
    row_scale = row_ramp * jnp.exp(jax.random.uniform(key_rows, (ROWS,), jnp.float32, 0.0, spread))
    col_scale = col_ramp * jnp.exp(jax.random.uniform(key_cols, (COLUMNS,), jnp.float32, 0.0, spread))
    cell_scale = jax.random.uniform(key_cells, (ROWS, COLUMNS), jnp.float32, floor_value, 1.0)
    return row_scale[:, None] * col_scale[None, :] * cell_scale / 40.0


def steps_of(own_key, dims, shards, least, top_value):
    factor_of = 1.0
    for dim, parts in shards:
        heights = jax.random.uniform(jax.random.fold_in(jax.random.fold_in(own_key, 6), dim), (parts,), jnp.float32, least / len(shards), top_value / len(shards))
        factor_of = factor_of * jnp.repeat(jnp.exp(heights), dims[dim] // parts).reshape((-1,) + (1,) * (len(dims) - 1 - dim))
    return factor_of


def normal_values(own_key, dims, scale, reach, cuts=(), kind=jnp.bfloat16):
    array = scale * jax.random.normal(own_key, dims, jnp.float32)
    if cuts:
        array = array * steps_of(own_key, dims, cuts, -0.22, 0.18)
    return jnp.clip(array, -reach, reach).astype(kind)


def setup_inputs(seed: int = 0) -> dict:
    key_of = jax.random.split(jax.random.key(seed), 5)
    return {
        "mask_logits": normal_values(key_of[0], (ROWS, COLUMNS), 1.5, 6.0, ((0, 32), (1, 16)), jnp.float32),
        "target": jnp.clip(1.0 * jax.random.uniform(key_of[1], (ROWS, COLUMNS), jnp.float32) ** steps_of(key_of[1], (ROWS, COLUMNS), ((0, 32), (1, 16)), -0.2, 0.2), 0.0, 1.0),
        "weight": draw_weight(jax.random.fold_in(key_of[4], 71), 0),
        "kernels": normal_values(key_of[3], (CONDITIONS, BANK_SIZE), 0.5, 3.0, ((1, 512),), jnp.float32),
    }


SHARPNESS = 6.0
THRESHOLD = 0.75
STEP = 0.5
EPSILON = 1e-06
DOSES = (1.0, 1.15)

def matmul(first, second):
    return jnp.matmul(first, second, precision=lax.Precision.HIGHEST, preferred_element_type=jnp.float32)

def cmatmul(first_re, first_im, second_re, second_im):
    return (matmul(first_re, second_re) - matmul(first_im, second_im), matmul(first_re, second_im) + matmul(first_im, second_re))

def dft_rows(band, pad_width):
    freq = jnp.arange(band, dtype=jnp.int32) - band // 2
    place = jnp.arange(pad_width, dtype=jnp.int32)
    turns = (freq[:, None] * place[None, :] % pad_width).astype(jnp.float32) * (2.0 * math.pi / pad_width)
    factor = 1.0 / math.sqrt(pad_width)
    return (jnp.cos(turns) * factor, -jnp.sin(turns) * factor)

def synthesize(spec_re, spec_im, wave_re, wave_im):
    left_re, left_im = cmatmul(wave_re.T, -wave_im.T, spec_re, spec_im)
    return cmatmul(left_re, left_im, wave_re, -wave_im)

def analyse(cell_re, cell_im, wave_re, wave_im):
    left_re, left_im = cmatmul(wave_re, wave_im, cell_re, cell_im)
    return cmatmul(left_re, left_im, wave_re.T, wave_im.T)

def tile_terms(padded_tile, kernel_re, kernel_im, wave_re, wave_im, dose, margin):
    mask_tile, target_tile, weight_tile = (padded_tile[0], padded_tile[1], padded_tile[2])
    pad_width = mask_tile.shape[0]
    core_width = pad_width - 2 * margin
    four_re, four_im = cmatmul(matmul(wave_re, mask_tile), matmul(wave_im, mask_tile), wave_re.T, wave_im.T)
    prod_re = four_re[None] * kernel_re - four_im[None] * kernel_im
    prod_im = four_re[None] * kernel_im + four_im[None] * kernel_re
    fields_re, fields_im = synthesize(prod_re, prod_im, wave_re, wave_im)
    intensity = lax.optimization_barrier(jnp.sum(fields_re * fields_re + fields_im * fields_im, axis=0))
    resist = jax.nn.sigmoid(SHARPNESS * (dose * intensity - THRESHOLD))
    error_map = resist - target_tile
    inner = (weight_tile * error_map * error_map)[margin:margin + core_width, margin:margin + core_width]
    tile_loss = jnp.sum(inner)
    slope_map = 2.0 * SHARPNESS * dose * weight_tile * error_map * resist * (1.0 - resist)
    back_re, back_im = analyse(slope_map[None] * fields_re, slope_map[None] * fields_im, wave_re, wave_im)
    sum_re = lax.optimization_barrier(jnp.sum(kernel_re * back_re + kernel_im * back_im, axis=0))
    sum_im = lax.optimization_barrier(jnp.sum(kernel_re * back_im - kernel_im * back_re, axis=0))
    core_re = wave_re[:, margin:margin + core_width]
    core_im = wave_im[:, margin:margin + core_width]
    left_re, left_im = cmatmul(core_re.T, -core_im.T, sum_re, sum_im)
    real_part = matmul(left_re, core_re) + matmul(left_im, core_im)
    return (2.0 * real_part, tile_loss)

def reference(mask_logits, target, weight, kernels):
    mask_cells = jax.nn.sigmoid(mask_logits)
    stacked = jnp.pad(jnp.stack([mask_cells, target, weight]), ((0, 0), (HALO, HALO), (HALO, HALO)))
    wave_re, wave_im = dft_rows(BAND, PAD)
    banks = kernels.reshape(CONDITIONS, 2, KERNELS, BAND, BAND)
    tile_rows = ROWS // CORE
    tile_cols = COLUMNS // CORE

    def one_tile(tile_index):
        row_start = tile_index // tile_cols * CORE
        col_start = tile_index % tile_cols * CORE
        padded_tile = lax.dynamic_slice(stacked, (jnp.int32(0), row_start.astype(jnp.int32), col_start.astype(jnp.int32)), (3, PAD, PAD))
        grad_tile = jnp.zeros((CORE, CORE), jnp.float32)
        loss_tile = jnp.float32(0.0)
        for condition in range(CONDITIONS):
            part_grad, part_loss = tile_terms(padded_tile, banks[condition, 0], banks[condition, 1], wave_re, wave_im, DOSES[condition], HALO)
            grad_tile = grad_tile + part_grad
            loss_tile = loss_tile + part_loss
        return (grad_tile, loss_tile)
    tile_grads, tile_losses = lax.map(one_tile, jnp.arange(tile_rows * tile_cols, dtype=jnp.int32))
    grad_cells = tile_grads.reshape(tile_rows, tile_cols, CORE, CORE).transpose(0, 2, 1, 3).reshape(ROWS, COLUMNS)
    grad_cells = grad_cells * mask_cells * (1.0 - mask_cells)
    cell_count = ROWS * COLUMNS
    loss_value = jnp.sum(tile_losses) / cell_count
    norm_value = jnp.sqrt(jnp.sum(grad_cells * grad_cells) / cell_count + EPSILON)
    return (mask_logits - STEP * grad_cells / norm_value, loss_value)
```

```python
import functools

import numpy as np
import ml_dtypes

import jax
import jax.numpy as jnp
from jax import lax
from jax.experimental import pallas as pl
from jax.experimental.pallas import tpu as pltpu
from jax.sharding import PartitionSpec as P

MESH = pl.DeviceIdType.MESH
F32 = jnp.float32
BF16 = jnp.bfloat16
DOSES = (1.0, 1.15)
EPSILON = 1e-06
CELLS = 4096 * 2048
GRID = 64
ROWS_H = 384


def tables():
    place = np.concatenate([np.arange(64, 192), np.arange(192, 256), np.arange(0, 64)])
    freq = np.arange(32) - 16

    def wave(points):
        turn = 2 * np.pi * ((freq[:, None] * points[None, :]) % 256) / 256
        return np.cos(turn) / 16, np.sin(turn) / 16

    cos_p, sin_p = wave(place)
    cos_g, sin_g = wave(4 * np.arange(GRID))
    out = {}
    mask_re = np.concatenate([cos_p.T, -sin_p.T], 1)
    mask_im = np.concatenate([sin_p.T, cos_p.T], 1)
    out["first"] = np.concatenate([mask_re, mask_re, mask_im, mask_im], 1)
    out["second"] = np.concatenate([cos_p, sin_p], 0)
    line, block = np.divmod(np.arange(ROWS_H), 128)
    core, y, part, low = block // 64, block // 8 % 8, block // 4 % 2, block % 4
    number = 3 * ((y * 2 + core) * 4 + low) + line
    kernel, u = number // 32, number % 32
    out["pick"] = (u[:, None] == np.arange(32)[None, :]).astype(np.float64)
    left_c = np.where(part[:, None] == 0, cos_g[u], -sin_g[u])
    left_d = np.where(part[:, None] == 0, sin_g[u], cos_g[u])
    out["left"] = np.concatenate([left_c, left_d], 0).T
    out["left_t"] = np.concatenate([left_c, left_c, left_d, left_d], 1)
    same = kernel[:, None] == np.arange(6)[None, :]
    out["own"] = np.concatenate([np.tile(same.T, (1, 2)), np.zeros((2, 768))], 0)
    out["own_t"] = np.repeat(same, 64, axis=1).astype(np.float64)
    zero = np.zeros((64, 128))
    right = np.concatenate(
        [np.concatenate([cos_g, sin_g], 1), np.concatenate([-sin_g, cos_g], 1)], 0
    )
    out["right"] = np.concatenate(
        [np.concatenate([right, zero], 1), np.concatenate([zero, right], 1)], 0
    )
    gap = place[:, None] - 4 * np.arange(GRID)[None, :]
    order = np.arange(1, 32)
    spread = (1 + 2 * np.cos(2 * np.pi * (gap[..., None] * order % 256) / 256).sum(-1)) / 64
    out["up_cols"] = np.concatenate([spread.T, spread.T], 0)
    out["up_rows"] = spread
    out["down_rows"] = spread.T
    out["down_cols"] = np.concatenate([spread, spread], 1)
    back = np.concatenate(
        [np.concatenate([cos_g.T, -sin_g.T], 1), np.concatenate([sin_g.T, cos_g.T], 1)], 0
    )
    turned = np.concatenate(
        [np.concatenate([-sin_g.T, -cos_g.T], 1), np.concatenate([cos_g.T, -sin_g.T], 1)], 0
    )
    zero = np.zeros((128, 64))
    out["back"] = np.concatenate(
        [
            np.concatenate([back, zero, turned, zero], 1),
            np.concatenate([zero, back, zero, turned], 1),
        ],
        0,
    )
    cos_c, sin_c = cos_p[:, :128], sin_p[:, :128]
    out["last_rows"] = np.concatenate([cos_c.T[:, u], sin_c.T[:, u]], 0)
    out["last_cols"] = 2 * np.concatenate(
        [cos_c, -sin_c, cos_c, -sin_c, -sin_c, -cos_c, -sin_c, -cos_c], 0
    )
    return out


SPLIT = (
    "first", "second", "right", "up_cols", "up_rows", "down_rows", "down_cols",
    "back", "last_rows", "last_cols",
)
PLAIN = ("left", "left_t", "own", "own_t")


def const_arrays():
    made = tables()
    names, arrays = [], []
    for name in SPLIT:
        value = made[name].astype(np.float32)
        high = value.astype(ml_dtypes.bfloat16)
        low = (value - high.astype(np.float32)).astype(ml_dtypes.bfloat16)
        names += [name + "_hi", name + "_lo"]
        arrays += [high, low]
    for name in PLAIN:
        names.append(name)
        arrays.append(made[name].astype(np.float32))
    names.append("pick")
    arrays.append(made["pick"].astype(ml_dtypes.bfloat16))
    return names, arrays


def split(value):
    high = value.astype(BF16)
    return high, (value - high.astype(F32)).astype(BF16)


def dot(first, second):
    return jnp.dot(first, second, preferred_element_type=F32)


def mm(first, second):
    return dot(first[0], second[0]) + (dot(first[1], second[0]) + dot(first[0], second[1]))


def build_left(k, left, own):
    return split(left * own[k : k + 1, :])


def spectrum(mask, con):
    half = mm(split(mask), con("first"))
    both = mm(con("second"), split(half))
    plain = both[:32, :128] - both[32:, 128:]
    turned = both[:32, 128:] + both[32:, :128]
    high, low = split(jnp.concatenate([plain, turned], axis=1))
    return dot(con.one("pick"), high) + dot(con.one("pick"), low)


def spread_bank(bank):
    lane = lax.broadcasted_iota(jnp.int32, (128, 128), 1)
    out = []
    for line in range(3):
        rolls = []
        for slot in range(4):
            shift = (32 * slot - 32 * line) % 128
            value = bank[slot // 2]
            rolls.append(value if shift == 0 else pltpu.roll(value, shift, 1))
        low = jnp.where(lane < 32, rolls[0], rolls[1])
        high = jnp.where(lane < 96, rolls[2], rolls[3])
        out.append(jnp.where(lane < 64, low, high))
    return jnp.concatenate(out, axis=0)


def fields_of(spec, bank, con, left):
    first = bank * spec[:, :128]
    second = bank * spec[:, 128:]
    lines = mm(left, split(jnp.concatenate([first, second], axis=0)))
    return mm(split(lines), con("right"))


def intensity_of(fields, con):
    square = fields * fields
    total = square[:64]
    for k in range(1, 6):
        total = total + square[64 * k : 64 * k + 64]
    stacked = jnp.concatenate([total[:, :128], total[:, 128:]], axis=0)
    wide = split(mm(split(stacked), con("up_cols")))
    return [mm(con("up_rows"), (wide[0][64 * c : 64 * c + 64], wide[1][64 * c : 64 * c + 64])) for c in range(2)]


def slope_of(intensity, target, weight, dose):
    resist = jax.nn.sigmoid(6.0 * (dose * intensity - 0.75))
    error = resist - target
    scaled = weight * error
    slope = (12.0 * dose) * scaled * resist * (1.0 - resist)
    return slope, (scaled * error)[:128, :128]


def gradient_of(slopes, fields, bank, con, left_t):
    rows = [mm(con("down_rows"), split(slope)) for slope in slopes]
    down = mm(split(jnp.concatenate(rows, axis=0)), con("down_cols"))
    pair = jnp.concatenate([down[:64], down[64:]], axis=1)
    moved = fields * jnp.concatenate([pair] * 6, axis=0)
    lines = mm(split(moved), con("back"))
    stacked = jnp.concatenate([lines[:, :128], lines[:, 128:]], axis=0)
    terms = bank * mm(left_t, split(stacked))
    last = mm(con("last_rows"), split(terms))
    return mm(split(jnp.concatenate([last[:128], last[128:]], axis=1)), con("last_cols"))


class Consts:
    def __init__(self, refs):
        self.refs = refs

    def __call__(self, name):
        return self.refs[name + "_hi"][...], self.refs[name + "_lo"][...]

    def one(self, name):
        return self.refs[name][...]


def kernel(names, *args):
    count = len(names)
    logits_ref, target_ref, weight_ref, bank_ref = args[:4]
    const_hbm = args[4 : 4 + count]
    out_ref, loss_ref = args[4 + count : 6 + count]
    const_vmem = args[6 + count : 6 + 2 * count]
    (
        left_hi, left_lo, left_t_hi, left_t_lo, vert, from_left, from_right,
        x_buf, z_send, z_buf, y_send, h_buf, r_send, r_buf,
        c_sem, vs_sem, vr_sem, hs_sem, hr_sem, es_sem, er_sem,
        xs_sem, xr_sem, zs_sem, zr_sem, ys_sem, yr_sem, rs_sem, rr_sem,
    ) = args[6 + 2 * count :]

    row = lax.axis_index("row")
    col = lax.axis_index("col")
    core = row % 2
    y = row // 2 % 8
    z_hi = row // 16
    z_lo = col // 4
    x = col % 4
    z = z_hi * 4 + z_lo

    def at(z_, y_, core_, x_):
        return ((z_ // 4 * 8 + y_) * 2 + core_, z_ % 4 * 4 + x_)

    x_peers = [at(z, y, core, (x + d) % 4) for d in range(1, 4)]
    xc_peers = [at(z, y, (core + e) % 2, (x + d) % 4) for d in range(4) for e in range(2) if d + e]
    z_peers = [at((z + d) % 8, y, core, x) for d in range(1, 8)]
    yc_peers = [at(z, (y + d) % 8, (core + e) % 2, x) for d in range(8) for e in range(2) if d + e]
    y_peers = [at(z, (y + d) % 8, core, x) for d in range(1, 8)]
    sides = [
        (row > 0, (row - 1, col)),
        (row < 31, (row + 1, col)),
        (col > 0, (row, col - 1)),
        (col < 15, (row, col + 1)),
    ]

    const_copies = [
        pltpu.make_async_copy(const_hbm[i], const_vmem[i], c_sem.at[i]) for i in range(count)
    ]
    for copy in const_copies:
        copy.start()

    for a in range(3):
        value = -1000.0 if a == 0 else 0.0
        vert[a] = jnp.full((128, 128), value, F32)
        from_left[a] = jnp.full((256, 128), value, F32)
        from_right[a] = jnp.full((256, 128), value, F32)

    barrier = pltpu.get_barrier_semaphore()
    for peer in xc_peers + z_peers + yc_peers:
        pl.semaphore_signal(barrier, inc=1, device_id=peer, device_id_type=MESH)
    waits = 29
    for there, peer in sides:
        @pl.when(there)
        def _():
            pl.semaphore_signal(barrier, inc=1, device_id=peer, device_id_type=MESH)
        waits = waits + there.astype(jnp.int32)

    for copy in const_copies:
        copy.wait()
    con = Consts(dict(zip(names, const_vmem)))
    left = con.one("left")
    own = con.one("own")
    for k in range(6):
        high, low = build_left(k, left, own)
        left_hi[64 * k : 64 * k + 64, :] = high
        left_lo[64 * k : 64 * k + 64, :] = low
    for part in range(2):
        table = con.one("left_t")[:, 128 * part : 128 * part + 128]
        for pair in range(3):
            mask = con.one("own_t")[:, 128 * pair : 128 * pair + 128]
            high, low = split(table * mask)
            where = 384 * part + 128 * pair
            left_t_hi[:, where : where + 128] = high
            left_t_lo[:, where : where + 128] = low

    pl.semaphore_wait(barrier, waits)

    def remote(src, dst, send, recv, peer):
        return pltpu.make_async_remote_copy(
            src_ref=src, dst_ref=dst, send_sem=send, recv_sem=recv,
            device_id=peer, device_id_type=MESH,
        )

    x_copies = [
        remote(bank_ref, x_buf.at[x], xs_sem.at[i], xr_sem.at[i], peer)
        for i, peer in enumerate(x_peers)
    ]
    for copy in x_copies:
        copy.start()
    x_buf[x] = bank_ref[...]

    sources = (logits_ref, target_ref, weight_ref)
    v_copies, h_copies, e_copies = [], [], []
    for a in range(3):
        v_copies.append([
            (sides[s][0], sides[1 - s][0], remote(
                sources[a].at[pl.ds(64 * s, 64)], vert.at[a, pl.ds(64 * s, 64)],
                vs_sem.at[a, s], vr_sem.at[a, s], sides[s][1]))
            for s in range(2)
        ])
        h_copies.append([
            (sides[2 + s][0], sides[3 - s][0], remote(
                sources[a], (from_right, from_left)[s].at[a, pl.ds(0, 128)],
                hs_sem.at[a, s], hr_sem.at[a, s], sides[2 + s][1]))
            for s in range(2)
        ])
        e_copies.append([
            (sides[2 + s][0], sides[3 - s][0], remote(
                vert.at[a], (from_right, from_left)[s].at[a, pl.ds(128, 128)],
                es_sem.at[a, s], er_sem.at[a, s], sides[2 + s][1]))
            for s in range(2)
        ])

    def start(group):
        for sends, _, copy in group:
            @pl.when(sends)
            def _():
                copy.start()

    def arrive(group):
        for _, comes, copy in group:
            @pl.when(comes)
            def _():
                copy.wait_recv()

    def sent(group):
        for sends, _, copy in group:
            @pl.when(sends)
            def _():
                copy.wait_send()

    start(v_copies[0])
    start(h_copies[0])
    start(v_copies[1])
    start(v_copies[2])

    for copy in x_copies:
        copy.wait_recv()
    joined = jnp.concatenate(
        [x_buf[0], x_buf[1], x_buf[2], x_buf[3], jnp.zeros((2, 32), F32)], axis=1
    )
    z_send[...] = joined
    z_copies = [
        remote(z_send, z_buf.at[z], zs_sem.at[i], zr_sem.at[i], peer)
        for i, peer in enumerate(z_peers)
    ]
    for copy in z_copies:
        copy.start()
    z_buf[z] = joined

    start(h_copies[1])
    start(h_copies[2])
    arrive(v_copies[0])
    start(e_copies[0])

    for copy in z_copies:
        copy.wait_recv()
    for c in range(2):
        y_send[c] = jnp.concatenate([z_buf[i, c : c + 1, :] for i in range(8)], axis=0)
    mine = core * 8 + y
    y_copies = [
        remote(y_send, h_buf.at[mine], ys_sem.at[i], yr_sem.at[i], peer)
        for i, peer in enumerate(yc_peers)
    ]
    for copy in y_copies:
        copy.start()
    h_buf[mine] = y_send[...]

    for a in (1, 2):
        arrive(v_copies[a])
        start(e_copies[a])

    def padded(a, own_ref):
        first = jnp.concatenate([own_ref[...], vert[a]], axis=0)
        lane = lax.broadcasted_iota(jnp.int32, (256, 128), 1)
        second = jnp.where(lane < 64, from_right[a], from_left[a])
        return jnp.concatenate([first, second], axis=1)

    arrive(h_copies[0])
    arrive(e_copies[0])
    spec = spectrum(jax.nn.sigmoid(padded(0, logits_ref)), con)

    for copy in y_copies:
        copy.wait_recv()
    bank = spread_bank([h_buf[:, c].reshape(128, 128) for c in range(2)])
    fields = fields_of(spec, bank, con, (left_hi[...], left_lo[...]))
    intensity = intensity_of(fields, con)

    for a in (1, 2):
        arrive(h_copies[a])
        arrive(e_copies[a])
    goal = padded(1, target_ref)
    weight = padded(2, weight_ref)
    slopes, losses = [], 0.0
    for c in range(2):
        slope, loss = slope_of(intensity[c], goal, weight, DOSES[c])
        slopes.append(slope)
        losses = losses + loss
    grad = gradient_of(slopes, fields, bank, con, (left_t_hi[...], left_t_lo[...]))
    logits = logits_ref[...]
    mask = jax.nn.sigmoid(logits)
    grad = grad * mask * (1.0 - mask)

    total = jnp.concatenate(
        [jnp.sum(grad * grad, axis=0, keepdims=True), jnp.sum(losses, axis=0, keepdims=True)],
        axis=0,
    )
    slot = 0
    r_copies = []
    for stage, peers in enumerate((xc_peers, z_peers, y_peers)):
        r_send[stage] = total
        copies = [
            remote(r_send.at[stage], r_buf.at[slot + i], rs_sem.at[slot + i], rr_sem.at[slot + i], peer)
            for i, peer in enumerate(peers)
        ]
        for copy in copies:
            copy.start()
        for copy in copies:
            copy.wait_recv()
        for i in range(len(peers)):
            total = total + r_buf[slot + i]
        slot += len(peers)
        r_copies += copies

    squares = jnp.sum(total[0:1, :], axis=1, keepdims=True)
    loss_ref[0, 0] = jnp.sum(total[1:2, :]) / CELLS
    norm = jnp.sqrt(squares / CELLS + EPSILON)
    out_ref[...] = logits - 0.5 * grad / norm

    for a in range(3):
        sent(v_copies[a])
        sent(h_copies[a])
        sent(e_copies[a])
    for copy in x_copies + z_copies + y_copies + r_copies:
        copy.wait_send()


def shards(mask_logits, target, weight, kernels):
    names, arrays = const_arrays()
    count = len(names)
    vmem = pl.BlockSpec(memory_space=pltpu.VMEM)
    dma = pltpu.SemaphoreType.DMA
    scratch = [pltpu.VMEM(a.shape, a.dtype) for a in arrays] + [
        pltpu.VMEM((384, 768), BF16), pltpu.VMEM((384, 768), BF16),
        pltpu.VMEM((384, 768), BF16), pltpu.VMEM((384, 768), BF16),
        pltpu.VMEM((3, 128, 128), F32),
        pltpu.VMEM((3, 256, 128), F32), pltpu.VMEM((3, 256, 128), F32),
        pltpu.VMEM((4, 2, 24), F32),
        pltpu.VMEM((2, 128), F32), pltpu.VMEM((8, 2, 128), F32),
        pltpu.VMEM((2, 8, 128), F32), pltpu.VMEM((16, 2, 8, 128), F32),
        pltpu.VMEM((3, 2, 128), F32), pltpu.VMEM((21, 2, 128), F32),
        dma((count,)), dma((3, 2)), dma((3, 2)), dma((3, 2)), dma((3, 2)), dma((3, 2)), dma((3, 2)),
        dma((3,)), dma((3,)), dma((7,)), dma((7,)), dma((15,)), dma((15,)), dma((21,)), dma((21,)),
    ]
    new_logits, loss = pl.pallas_call(
        functools.partial(kernel, names),
        out_shape=(
            jax.ShapeDtypeStruct((128, 128), F32),
            jax.ShapeDtypeStruct((1, 1), F32),
        ),
        in_specs=[vmem] * 4 + [pl.BlockSpec(memory_space=pl.ANY)] * count,
        out_specs=(vmem, pl.BlockSpec(memory_space=pltpu.SMEM)),
        scratch_shapes=scratch,
        compiler_params=pltpu.CompilerParams(collective_id=0, has_side_effects=True),
        name="litho",
    )(mask_logits, target, weight, kernels, *[jnp.asarray(a) for a in arrays])
    return new_logits, loss.reshape(())


def solution(mesh):
    placed = (P("row", "col"), P("row", "col"), P("row", "col"), P(None, ("row", "col")))
    return jax.shard_map(
        shards, mesh=mesh, in_specs=placed, out_specs=(P("row", "col"), P()), check_vma=False
    )
```

```python
import functools

import numpy as np
import ml_dtypes

import jax
import jax.numpy as jnp
from jax import lax
from jax.experimental import pallas as pl
from jax.experimental.pallas import tpu as pltpu
from jax.sharding import PartitionSpec as P

MESH = pl.DeviceIdType.MESH
F32 = jnp.float32
BF16 = jnp.bfloat16
DOSES = (1.0, 1.15)
EPSILON = 1e-06
CELLS = 4096 * 2048
GRID = 64
ROWS_H = 384


def tables():
    place = np.concatenate([np.arange(64, 192), np.arange(192, 256), np.arange(0, 64)])
    freq = np.arange(32) - 16

    def wave(points):
        turn = 2 * np.pi * ((freq[:, None] * points[None, :]) % 256) / 256
        return np.cos(turn) / 16, np.sin(turn) / 16

    cos_p, sin_p = wave(place)
    cos_g, sin_g = wave(4 * np.arange(GRID))
    out = {}
    mask_re = np.concatenate([cos_p.T, -sin_p.T], 1)
    mask_im = np.concatenate([sin_p.T, cos_p.T], 1)
    out["first"] = np.concatenate([mask_re, mask_re, mask_im, mask_im], 1)
    out["second"] = np.concatenate([cos_p, sin_p], 0)
    line, block = np.divmod(np.arange(ROWS_H), 128)
    core, y, part, low = block // 64, block // 8 % 8, block // 4 % 2, block % 4
    number = 3 * ((y * 2 + core) * 4 + low) + line
    kernel, u = number // 32, number % 32
    out["pick"] = (u[:, None] == np.arange(32)[None, :]).astype(np.float64)
    left_c = np.where(part[:, None] == 0, cos_g[u], -sin_g[u])
    left_d = np.where(part[:, None] == 0, sin_g[u], cos_g[u])
    out["left"] = np.concatenate([left_c, left_d], 0).T
    out["left_t"] = np.concatenate([left_c, left_c, left_d, left_d], 1)
    same = kernel[:, None] == np.arange(6)[None, :]
    out["own"] = np.concatenate([np.tile(same.T, (1, 2)), np.zeros((2, 768))], 0)
    out["own_t"] = np.repeat(same, 64, axis=1).astype(np.float64)
    zero = np.zeros((64, 128))
    right = np.concatenate(
        [np.concatenate([cos_g, sin_g], 1), np.concatenate([-sin_g, cos_g], 1)], 0
    )
    out["right"] = np.concatenate(
        [np.concatenate([right, zero], 1), np.concatenate([zero, right], 1)], 0
    )
    gap = place[:, None] - 4 * np.arange(GRID)[None, :]
    order = np.arange(1, 32)
    spread = (1 + 2 * np.cos(2 * np.pi * (gap[..., None] * order % 256) / 256).sum(-1)) / 64
    out["up_cols"] = np.concatenate([spread.T, spread.T], 0)
    out["up_rows"] = spread
    out["down_rows"] = spread.T
    out["down_cols"] = np.concatenate([spread, spread], 1)
    back = np.concatenate(
        [np.concatenate([cos_g.T, -sin_g.T], 1), np.concatenate([sin_g.T, cos_g.T], 1)], 0
    )
    turned = np.concatenate(
        [np.concatenate([-sin_g.T, -cos_g.T], 1), np.concatenate([cos_g.T, -sin_g.T], 1)], 0
    )
    zero = np.zeros((128, 64))
    out["back"] = np.concatenate(
        [
            np.concatenate([back, zero, turned, zero], 1),
            np.concatenate([zero, back, zero, turned], 1),
        ],
        0,
    )
    cos_c, sin_c = cos_p[:, :128], sin_p[:, :128]
    out["last_rows"] = np.concatenate([cos_c.T[:, u], sin_c.T[:, u]], 0)
    out["last_cols"] = 2 * np.concatenate(
        [cos_c, -sin_c, cos_c, -sin_c, -sin_c, -cos_c, -sin_c, -cos_c], 0
    )
    return out


SPLIT = (
    "first", "second", "right", "up_cols", "up_rows", "down_rows", "down_cols",
    "back", "last_rows", "last_cols",
)
PLAIN = ("left", "left_t", "own", "own_t")


def const_arrays():
    made = tables()
    names, arrays = [], []
    for name in SPLIT:
        value = made[name].astype(np.float32)
        high = value.astype(ml_dtypes.bfloat16)
        low = (value - high.astype(np.float32)).astype(ml_dtypes.bfloat16)
        names += [name + "_hi", name + "_lo"]
        arrays += [high, low]
    for name in PLAIN:
        names.append(name)
        arrays.append(made[name].astype(np.float32))
    names.append("pick")
    arrays.append(made["pick"].astype(ml_dtypes.bfloat16))
    return names, arrays


def split(value):
    high = value.astype(BF16)
    return high, (value - high.astype(F32)).astype(BF16)


def dot(first, second):
    return jnp.dot(first, second, preferred_element_type=F32)


def mm(first, second):
    return dot(first[0], second[0]) + (dot(first[1], second[0]) + dot(first[0], second[1]))


def build_left(k, left, own):
    return split(left * own[k : k + 1, :])


def spectrum(mask, con):
    half = mm(split(mask), con("first"))
    both = mm(con("second"), split(half))
    plain = both[:32, :128] - both[32:, 128:]
    turned = both[:32, 128:] + both[32:, :128]
    high, low = split(jnp.concatenate([plain, turned], axis=1))
    return dot(con.one("pick"), high) + dot(con.one("pick"), low)


def spread_bank(bank):
    lane = lax.broadcasted_iota(jnp.int32, (128, 128), 1)
    out = []
    for line in range(3):
        rolls = []
        for slot in range(4):
            shift = (32 * slot - 32 * line) % 128
            value = bank[slot // 2]
            rolls.append(value if shift == 0 else pltpu.roll(value, shift, 1))
        low = jnp.where(lane < 32, rolls[0], rolls[1])
        high = jnp.where(lane < 96, rolls[2], rolls[3])
        out.append(jnp.where(lane < 64, low, high))
    return jnp.concatenate(out, axis=0)


def fields_of(spec, bank, con, left):
    first = bank * spec[:, :128]
    second = bank * spec[:, 128:]
    lines = mm(left, split(jnp.concatenate([first, second], axis=0)))
    return mm(split(lines), con("right"))


def intensity_of(fields, con):
    square = fields * fields
    total = square[:64]
    for k in range(1, 6):
        total = total + square[64 * k : 64 * k + 64]
    stacked = jnp.concatenate([total[:, :128], total[:, 128:]], axis=0)
    wide = split(mm(split(stacked), con("up_cols")))
    return [mm(con("up_rows"), (wide[0][64 * c : 64 * c + 64], wide[1][64 * c : 64 * c + 64])) for c in range(2)]


def slope_of(intensity, target, weight, dose):
    resist = jax.nn.sigmoid(6.0 * (dose * intensity - 0.75))
    error = resist - target
    scaled = weight * error
    slope = (12.0 * dose) * scaled * resist * (1.0 - resist)
    return slope, (scaled * error)[:128, :128]


def gradient_of(slopes, fields, bank, con, left_t):
    rows = [mm(con("down_rows"), split(slope)) for slope in slopes]
    down = mm(split(jnp.concatenate(rows, axis=0)), con("down_cols"))
    pair = jnp.concatenate([down[:64], down[64:]], axis=1)
    moved = fields * jnp.concatenate([pair] * 6, axis=0)
    lines = mm(split(moved), con("back"))
    stacked = jnp.concatenate([lines[:, :128], lines[:, 128:]], axis=0)
    terms = bank * mm(left_t, split(stacked))
    last = mm(con("last_rows"), split(terms))
    return mm(split(jnp.concatenate([last[:128], last[128:]], axis=1)), con("last_cols"))


class Consts:
    def __init__(self, refs):
        self.refs = refs

    def __call__(self, name):
        return self.refs[name + "_hi"][...], self.refs[name + "_lo"][...]

    def one(self, name):
        return self.refs[name][...]


def kernel(names, *args):
    count = len(names)
    logits_ref, target_ref, weight_ref, bank_ref = args[:4]
    const_hbm = args[4 : 4 + count]
    out_ref, loss_ref = args[4 + count : 6 + count]
    const_vmem = args[6 + count : 6 + 2 * count]
    (
        left_hi, left_lo, left_t_hi, left_t_lo, vert, from_left, from_right,
        x_buf, y_send, h_buf, r_send, r_buf,
        c_sem, vs_sem, vr_sem, hs_sem, hr_sem, es_sem, er_sem,
        xs_sem, xr_sem, ys_sem, yr_sem, ps_sem, pr_sem, rs_sem, rr_sem,
    ) = args[6 + 2 * count :]

    row = lax.axis_index("row")
    col = lax.axis_index("col")
    core = row % 2
    y = row // 2 % 8
    z_hi = row // 16
    z_lo = col // 4
    x = col % 4
    z = z_hi * 4 + z_lo

    def at(z_, y_, core_, x_):
        return ((z_ // 4 * 8 + y_) * 2 + core_, z_ % 4 * 4 + x_)

    partner = at(z, y, 1 - core, x)
    xz_peers = [at((z + d) % 8, y, core, (x + e) % 4) for d in range(8) for e in range(4) if d + e]
    xzc_peers = [
        at((z + d) % 8, y, (core + f) % 2, (x + e) % 4)
        for d in range(8) for e in range(4) for f in range(2) if d + e + f
    ]
    y_peers = [at(z, (y + d) % 8, core, x) for d in range(1, 8)]
    sides = [
        (row > 0, (row - 1, col)),
        (row < 31, (row + 1, col)),
        (col > 0, (row, col - 1)),
        (col < 15, (row, col + 1)),
    ]

    barrier = pltpu.get_barrier_semaphore()
    for peer in [partner] + xz_peers + y_peers:
        pl.semaphore_signal(barrier, inc=1, device_id=peer, device_id_type=MESH)
    waits = 39
    for there, peer in sides:
        @pl.when(there)
        def _():
            pl.semaphore_signal(barrier, inc=1, device_id=peer, device_id_type=MESH)
        waits = waits + there.astype(jnp.int32)

    const_copies = [
        pltpu.make_async_copy(const_hbm[i], const_vmem[i], c_sem.at[i]) for i in range(count)
    ]
    for copy in const_copies:
        copy.start()

    def fill(ref):
        ref[...] = jnp.zeros(ref.shape, F32)
        ref[0] = jnp.full(ref.shape[1:], -1000.0, F32)

    for missing, ref in (
        (row == 0, vert.at[:, pl.ds(64, 64)]),
        (row == 31, vert.at[:, pl.ds(0, 64)]),
        (col == 0, from_left),
        (col == 15, from_right),
    ):
        @pl.when(missing)
        def _():
            fill(ref)

    pl.semaphore_wait(barrier, waits)

    def remote(src, dst, send, recv, peer):
        return pltpu.make_async_remote_copy(
            src_ref=src, dst_ref=dst, send_sem=send, recv_sem=recv,
            device_id=peer, device_id_type=MESH,
        )

    x_copies = [
        remote(bank_ref, x_buf.at[z, x], xs_sem.at[i], xr_sem.at[i], peer)
        for i, peer in enumerate(xz_peers)
    ]
    for copy in x_copies:
        copy.start()
    x_buf[z, x] = bank_ref[...]

    sources = (logits_ref, target_ref, weight_ref)
    v_copies, h_copies, e_copies = [], [], []
    for a in range(3):
        v_copies.append([
            (sides[s][0], sides[1 - s][0], remote(
                sources[a].at[pl.ds(64 * s, 64)], vert.at[a, pl.ds(64 * s, 64)],
                vs_sem.at[a, s], vr_sem.at[a, s], sides[s][1]))
            for s in range(2)
        ])
        h_copies.append([
            (sides[2 + s][0], sides[3 - s][0], remote(
                sources[a], (from_right, from_left)[s].at[a, pl.ds(0, 128)],
                hs_sem.at[a, s], hr_sem.at[a, s], sides[2 + s][1]))
            for s in range(2)
        ])
        e_copies.append([
            (sides[2 + s][0], sides[3 - s][0], remote(
                vert.at[a], (from_right, from_left)[s].at[a, pl.ds(128, 128)],
                es_sem.at[a, s], er_sem.at[a, s], sides[2 + s][1]))
            for s in range(2)
        ])

    def start(group):
        for sends, _, copy in group:
            @pl.when(sends)
            def _():
                copy.start()

    def arrive(group):
        for _, comes, copy in group:
            @pl.when(comes)
            def _():
                copy.wait_recv()

    def sent(group):
        for sends, _, copy in group:
            @pl.when(sends)
            def _():
                copy.wait_send()

    start(v_copies[0])
    start(h_copies[0])
    start(v_copies[1])
    start(v_copies[2])
    start(h_copies[1])
    start(h_copies[2])

    for copy in const_copies:
        copy.wait()
    con = Consts(dict(zip(names, const_vmem)))
    left = con.one("left")
    own = con.one("own")
    for k in range(6):
        high, low = build_left(k, left, own)
        left_hi[64 * k : 64 * k + 64, :] = high
        left_lo[64 * k : 64 * k + 64, :] = low
    for part in range(2):
        table = con.one("left_t")[:, 128 * part : 128 * part + 128]
        for pair in range(3):
            mask = con.one("own_t")[:, 128 * pair : 128 * pair + 128]
            high, low = split(table * mask)
            where = 384 * part + 128 * pair
            left_t_hi[:, where : where + 128] = high
            left_t_lo[:, where : where + 128] = low

    for copy in x_copies:
        copy.wait_recv()
    for c in range(2):
        parts = [
            jnp.concatenate([x_buf[i, p, c : c + 1, :] for i in range(8)], axis=0)
            for p in range(4)
        ]
        y_send[c] = jnp.concatenate(parts + [jnp.zeros((8, 32), F32)], axis=1)
    mine = core * 8 + y
    y_copies = [
        remote(y_send, h_buf.at[mine], ys_sem.at[i], yr_sem.at[i], peer)
        for i, peer in enumerate(y_peers)
    ]
    for copy in y_copies:
        copy.start()
    p_copies = [remote(y_send, h_buf.at[mine], ps_sem.at[0], pr_sem.at[0], partner)]
    p_copies[0].start()
    h_buf[mine] = y_send[...]

    arrive(v_copies[0])
    start(e_copies[0])
    for i in (0, 6, 1, 5, 2, 4, 3):
        y_copies[i].wait_recv()
        piece = h_buf.at[core * 8 + (y + 7 - i) % 8]
        p_copies.append(remote(piece, piece, ps_sem.at[1 + i], pr_sem.at[1 + i], partner))
        p_copies[-1].start()

    for a in (1, 2):
        arrive(v_copies[a])
        start(e_copies[a])

    def padded(a, own_ref):
        first = jnp.concatenate([own_ref[...], vert[a]], axis=0)
        lane = lax.broadcasted_iota(jnp.int32, (256, 128), 1)
        second = jnp.where(lane < 64, from_right[a], from_left[a])
        return jnp.concatenate([first, second], axis=1)

    arrive(h_copies[0])
    arrive(e_copies[0])
    spec = spectrum(jax.nn.sigmoid(padded(0, logits_ref)), con)

    for copy in p_copies:
        copy.wait_recv()
    bank = spread_bank([h_buf[:, c].reshape(128, 128) for c in range(2)])
    fields = fields_of(spec, bank, con, (left_hi[...], left_lo[...]))
    intensity = intensity_of(fields, con)

    for a in (1, 2):
        arrive(h_copies[a])
        arrive(e_copies[a])
    goal = padded(1, target_ref)
    weight = padded(2, weight_ref)
    slopes, losses = [], 0.0
    for c in range(2):
        slope, loss = slope_of(intensity[c], goal, weight, DOSES[c])
        slopes.append(slope)
        losses = losses + loss
    grad = gradient_of(slopes, fields, bank, con, (left_t_hi[...], left_t_lo[...]))
    logits = logits_ref[...]
    mask = jax.nn.sigmoid(logits)
    grad = grad * mask * (1.0 - mask)

    total = jnp.concatenate(
        [jnp.sum(grad * grad, axis=0, keepdims=True), jnp.sum(losses, axis=0, keepdims=True)],
        axis=0,
    )
    slot = 0
    r_copies = []
    for stage, peers in enumerate((xzc_peers, y_peers)):
        r_send[stage] = total
        copies = [
            remote(r_send.at[stage], r_buf.at[slot + i], rs_sem.at[slot + i], rr_sem.at[slot + i], peer)
            for i, peer in enumerate(peers)
        ]
        for copy in copies:
            copy.start()
        for copy in copies:
            copy.wait_recv()
        for i in range(len(peers)):
            total = total + r_buf[slot + i]
        slot += len(peers)
        r_copies += copies

    squares = jnp.sum(total[0:1, :], axis=1, keepdims=True)
    loss_ref[0, 0] = jnp.sum(total[1:2, :]) / CELLS
    norm = jnp.sqrt(squares / CELLS + EPSILON)
    out_ref[...] = logits - 0.5 * grad / norm

    for a in range(3):
        sent(v_copies[a])
        sent(h_copies[a])
        sent(e_copies[a])
    for copy in x_copies + y_copies + p_copies + r_copies:
        copy.wait_send()


def shards(mask_logits, target, weight, kernels):
    names, arrays = const_arrays()
    count = len(names)
    vmem = pl.BlockSpec(memory_space=pltpu.VMEM)
    dma = pltpu.SemaphoreType.DMA
    scratch = [pltpu.VMEM(a.shape, a.dtype) for a in arrays] + [
        pltpu.VMEM((384, 768), BF16), pltpu.VMEM((384, 768), BF16),
        pltpu.VMEM((384, 768), BF16), pltpu.VMEM((384, 768), BF16),
        pltpu.VMEM((3, 128, 128), F32),
        pltpu.VMEM((3, 256, 128), F32), pltpu.VMEM((3, 256, 128), F32),
        pltpu.VMEM((8, 4, 2, 24), F32),
        pltpu.VMEM((2, 8, 128), F32), pltpu.VMEM((16, 2, 8, 128), F32),
        pltpu.VMEM((2, 2, 128), F32), pltpu.VMEM((70, 2, 128), F32),
        dma((count,)), dma((3, 2)), dma((3, 2)), dma((3, 2)), dma((3, 2)), dma((3, 2)), dma((3, 2)),
        dma((31,)), dma((31,)), dma((7,)), dma((7,)), dma((8,)), dma((8,)), dma((70,)), dma((70,)),
    ]
    new_logits, loss = pl.pallas_call(
        functools.partial(kernel, names),
        out_shape=(
            jax.ShapeDtypeStruct((128, 128), F32),
            jax.ShapeDtypeStruct((1, 1), F32),
        ),
        in_specs=[vmem] * 4 + [pl.BlockSpec(memory_space=pl.ANY)] * count,
        out_specs=(vmem, pl.BlockSpec(memory_space=pltpu.SMEM)),
        scratch_shapes=scratch,
        compiler_params=pltpu.CompilerParams(collective_id=0, has_side_effects=True),
        name="litho",
    )(mask_logits, target, weight, kernels, *[jnp.asarray(a) for a in arrays])
    return new_logits, loss.reshape(())


def solution(mesh):
    placed = (P("row", "col"), P("row", "col"), P("row", "col"), P(None, ("row", "col")))
    return jax.shard_map(
        shards, mesh=mesh, in_specs=placed, out_specs=(P("row", "col"), P()), check_vma=False
    )
```

```python
import functools

import numpy as np
import ml_dtypes

import jax
import jax.numpy as jnp
from jax import lax
from jax.experimental import pallas as pl
from jax.experimental.pallas import tpu as pltpu
from jax.sharding import PartitionSpec as P

MESH = pl.DeviceIdType.MESH
F32 = jnp.float32
BF16 = jnp.bfloat16
DOSES = (1.0, 1.15)
EPSILON = 1e-06
CELLS = 4096 * 2048
GRID = 64
ROWS_H = 384


def tables():
    place = np.concatenate([np.arange(64, 192), np.arange(192, 256), np.arange(0, 64)])
    freq = np.arange(32) - 16

    def wave(points):
        turn = 2 * np.pi * ((freq[:, None] * points[None, :]) % 256) / 256
        return np.cos(turn) / 16, np.sin(turn) / 16

    cos_p, sin_p = wave(place)
    cos_g, sin_g = wave(4 * np.arange(GRID))
    out = {}
    mask_re = np.concatenate([cos_p.T, -sin_p.T], 1)
    mask_im = np.concatenate([sin_p.T, cos_p.T], 1)
    out["first"] = np.concatenate([mask_re, mask_re, mask_im, mask_im], 1)
    out["second"] = np.concatenate([cos_p, sin_p], 0)
    line, block = np.divmod(np.arange(ROWS_H), 128)
    core, y, part, low = block // 64, block // 8 % 8, block // 4 % 2, block % 4
    number = 3 * ((y * 2 + core) * 4 + low) + line
    kernel, u = number // 32, number % 32
    out["pick"] = (u[:, None] == np.arange(32)[None, :]).astype(np.float64)
    left_c = np.where(part[:, None] == 0, cos_g[u], -sin_g[u])
    left_d = np.where(part[:, None] == 0, sin_g[u], cos_g[u])
    out["left"] = np.concatenate([left_c, left_d], 0).T
    out["left_t"] = np.concatenate([left_c, left_c, left_d, left_d], 1)
    same = kernel[:, None] == np.arange(6)[None, :]
    out["own"] = np.concatenate([np.tile(same.T, (1, 2)), np.zeros((2, 768))], 0)
    out["own_t"] = np.repeat(same, 64, axis=1).astype(np.float64)
    zero = np.zeros((64, 128))
    right = np.concatenate(
        [np.concatenate([cos_g, sin_g], 1), np.concatenate([-sin_g, cos_g], 1)], 0
    )
    out["right"] = np.concatenate(
        [np.concatenate([right, zero], 1), np.concatenate([zero, right], 1)], 0
    )
    gap = place[:, None] - 4 * np.arange(GRID)[None, :]
    order = np.arange(1, 32)
    spread = (1 + 2 * np.cos(2 * np.pi * (gap[..., None] * order % 256) / 256).sum(-1)) / 64
    out["up_cols"] = np.concatenate([spread.T, spread.T], 0)
    out["up_rows"] = spread
    out["down_rows"] = spread.T
    out["down_cols"] = np.concatenate([spread, spread], 1)
    back = np.concatenate(
        [np.concatenate([cos_g.T, -sin_g.T], 1), np.concatenate([sin_g.T, cos_g.T], 1)], 0
    )
    turned = np.concatenate(
        [np.concatenate([-sin_g.T, -cos_g.T], 1), np.concatenate([cos_g.T, -sin_g.T], 1)], 0
    )
    zero = np.zeros((128, 64))
    out["back"] = np.concatenate(
        [
            np.concatenate([back, zero, turned, zero], 1),
            np.concatenate([zero, back, zero, turned], 1),
        ],
        0,
    )
    cos_c, sin_c = cos_p[:, :128], sin_p[:, :128]
    out["last_rows"] = np.concatenate([cos_c.T[:, u], sin_c.T[:, u]], 0)
    out["last_cols"] = 2 * np.concatenate(
        [cos_c, -sin_c, cos_c, -sin_c, -sin_c, -cos_c, -sin_c, -cos_c], 0
    )
    return out


SPLIT = (
    "first", "second", "right", "up_cols", "up_rows", "down_rows", "down_cols",
    "back", "last_rows", "last_cols",
)
PLAIN = ("left", "left_t", "own", "own_t")


def const_arrays():
    made = tables()
    names, arrays = [], []
    for name in SPLIT:
        value = made[name].astype(np.float32)
        high = value.astype(ml_dtypes.bfloat16)
        low = (value - high.astype(np.float32)).astype(ml_dtypes.bfloat16)
        names += [name + "_hi", name + "_lo"]
        arrays += [high, low]
    for name in PLAIN:
        names.append(name)
        arrays.append(made[name].astype(np.float32))
    names.append("pick")
    arrays.append(made["pick"].astype(ml_dtypes.bfloat16))
    return names, arrays


def split(value):
    high = value.astype(BF16)
    return high, (value - high.astype(F32)).astype(BF16)


def dot(first, second):
    return jnp.dot(first, second, preferred_element_type=F32)


def mm(first, second):
    return dot(first[0], second[0]) + (dot(first[1], second[0]) + dot(first[0], second[1]))


def build_left(k, left, own):
    return split(left * own[k : k + 1, :])


def spectrum(mask, con):
    half = mm(split(mask), con("first"))
    both = mm(con("second"), split(half))
    plain = both[:32, :128] - both[32:, 128:]
    turned = both[:32, 128:] + both[32:, :128]
    high, low = split(jnp.concatenate([plain, turned], axis=1))
    return dot(con.one("pick"), high) + dot(con.one("pick"), low)


def spread_bank(bank):
    lane = lax.broadcasted_iota(jnp.int32, (128, 128), 1)
    out = []
    for line in range(3):
        rolls = []
        for slot in range(4):
            shift = (32 * slot - 32 * line) % 128
            value = bank[slot // 2]
            rolls.append(value if shift == 0 else pltpu.roll(value, shift, 1))
        low = jnp.where(lane < 32, rolls[0], rolls[1])
        high = jnp.where(lane < 96, rolls[2], rolls[3])
        out.append(jnp.where(lane < 64, low, high))
    return jnp.concatenate(out, axis=0)


def fields_of(spec, bank, con, left):
    first = bank * spec[:, :128]
    second = bank * spec[:, 128:]
    lines = mm(left, split(jnp.concatenate([first, second], axis=0)))
    return mm(split(lines), con("right"))


def intensity_of(fields, con):
    square = fields * fields
    total = square[:64]
    for k in range(1, 6):
        total = total + square[64 * k : 64 * k + 64]
    stacked = jnp.concatenate([total[:, :128], total[:, 128:]], axis=0)
    wide = split(mm(split(stacked), con("up_cols")))
    return [mm(con("up_rows"), (wide[0][64 * c : 64 * c + 64], wide[1][64 * c : 64 * c + 64])) for c in range(2)]


def slope_of(intensity, target, weight, dose):
    resist = jax.nn.sigmoid(6.0 * (dose * intensity - 0.75))
    error = resist - target
    scaled = weight * error
    slope = (12.0 * dose) * scaled * resist * (1.0 - resist)
    return slope, (scaled * error)[:128, :128]


def gradient_of(slopes, fields, bank, con, left_t):
    rows = [mm(con("down_rows"), split(slope)) for slope in slopes]
    down = mm(split(jnp.concatenate(rows, axis=0)), con("down_cols"))
    pair = jnp.concatenate([down[:64], down[64:]], axis=1)
    moved = fields * jnp.concatenate([pair] * 6, axis=0)
    lines = mm(split(moved), con("back"))
    stacked = jnp.concatenate([lines[:, :128], lines[:, 128:]], axis=0)
    terms = bank * mm(left_t, split(stacked))
    last = mm(con("last_rows"), split(terms))
    return mm(split(jnp.concatenate([last[:128], last[128:]], axis=1)), con("last_cols"))


class Consts:
    def __init__(self, refs):
        self.refs = refs

    def __call__(self, name):
        return self.refs[name + "_hi"][...], self.refs[name + "_lo"][...]

    def one(self, name):
        return self.refs[name][...]


def kernel(names, *args):
    count = len(names)
    logits_ref, target_ref, weight_ref, bank_ref = args[:4]
    const_hbm = args[4 : 4 + count]
    out_ref, loss_ref = args[4 + count : 6 + count]
    const_vmem = args[6 + count : 6 + 2 * count]
    (
        left_hi, left_lo, left_t_hi, left_t_lo, vert, pack, from_left, from_right,
        x_buf, y_send, h_buf, r_send, r_buf,
        c_sem, vs_sem, vr_sem, hs_sem, hr_sem, es_sem, er_sem,
        xs_sem, xr_sem, ys_sem, yr_sem, rs_sem, rr_sem,
    ) = args[6 + 2 * count :]

    row = lax.axis_index("row")
    col = lax.axis_index("col")
    core = row % 2
    y = row // 2 % 8
    z_hi = row // 16
    z_lo = col // 4
    x = col % 4
    z = z_hi * 4 + z_lo

    def at(z_, y_, core_, x_):
        return ((z_ // 4 * 8 + y_) * 2 + core_, z_ % 4 * 4 + x_)

    xz_peers = [at((z + d) % 8, y, core, (x + e) % 4) for d in range(8) for e in range(4) if d + e]
    yc_peers = [at(z, (y + d) % 8, (core + e) % 2, x) for d in range(8) for e in range(2) if d + e]
    sides = [
        (row > 0, (row - 1, col)),
        (row < 31, (row + 1, col)),
        (col > 0, (row, col - 1)),
        (col < 15, (row, col + 1)),
    ]

    barrier = pltpu.get_barrier_semaphore()
    for peer in xz_peers + yc_peers:
        pl.semaphore_signal(barrier, inc=1, device_id=peer, device_id_type=MESH)
    waits = 46
    for there, peer in sides:
        @pl.when(there)
        def _():
            pl.semaphore_signal(barrier, inc=1, device_id=peer, device_id_type=MESH)
        waits = waits + there.astype(jnp.int32)

    const_copies = [
        pltpu.make_async_copy(const_hbm[i], const_vmem[i], c_sem.at[i]) for i in range(count)
    ]
    for copy in const_copies:
        copy.start()

    def fill_rows(first):
        vert[0, first : first + 64] = jnp.full((64, 128), -1000.0, F32)
        for a in (1, 2):
            vert[a, first : first + 64] = jnp.zeros((64, 128), F32)

    def fill_side(ref):
        ref[0:128] = jnp.full((128, 128), -1000.0, F32)
        ref[128:384] = jnp.zeros((256, 128), F32)

    for missing, fill, where in (
        (row == 0, fill_rows, 64),
        (row == 31, fill_rows, 0),
        (col == 0, fill_side, from_left),
        (col == 15, fill_side, from_right),
    ):
        @pl.when(missing)
        def _():
            fill(where)

    low_lanes = lax.broadcasted_iota(jnp.int32, (64, 128), 1) < 64
    low_pair = lax.broadcasted_iota(jnp.int32, (128, 128), 1) < 64

    def pack_logits(block, line):
        top, bottom = block[:64], block[64:]
        pack[0, line : line + 64] = jnp.where(low_lanes, top, pltpu.roll(bottom, 64, 1))
        pack[1, line : line + 64] = jnp.where(low_lanes, pltpu.roll(top, 64, 1), bottom)

    def unfolded(block):
        core_rows, margin = block[:64], block[64:]
        return [core_rows, pltpu.roll(core_rows, 64, 1), margin, pltpu.roll(margin, 64, 1)]

    def unfolded_high(block):
        core_rows, margin = block[:64], block[64:]
        return [pltpu.roll(core_rows, 64, 1), core_rows, pltpu.roll(margin, 64, 1), margin]

    def pack_pair(first, second, line):
        line = line + 128
        pack[0, line : line + 128] = jnp.where(low_pair, first, pltpu.roll(second, 64, 1))
        pack[1, line : line + 128] = jnp.where(low_pair, pltpu.roll(first, 64, 1), second)

    pack_logits(logits_ref[...], 0)
    pack_pair(target_ref[...], weight_ref[...], 0)

    pl.semaphore_wait(barrier, waits)

    def remote(src, dst, send, recv, peer):
        return pltpu.make_async_remote_copy(
            src_ref=src, dst_ref=dst, send_sem=send, recv_sem=recv,
            device_id=peer, device_id_type=MESH,
        )

    x_copies = [
        remote(bank_ref, x_buf.at[z, x], xs_sem.at[i], xr_sem.at[i], peer)
        for i, peer in enumerate(xz_peers)
    ]
    for copy in x_copies:
        copy.start()
    x_buf[z, x] = bank_ref[...]

    sources = (logits_ref, target_ref, weight_ref)
    v_copies = [
        [
            (sides[s][0], sides[1 - s][0], remote(
                sources[a].at[pl.ds(64 * s, 64)], vert.at[a, pl.ds(64 * s, 64)],
                vs_sem.at[a, s], vr_sem.at[a, s], sides[s][1]))
            for s in range(2)
        ]
        for a in range(3)
    ]

    def side_copies(lines, send, recv):
        return [
            (sides[2 + s][0], sides[3 - s][0], remote(
                pack.at[s, lines], (from_right, from_left)[s].at[lines],
                send.at[s], recv.at[s], sides[2 + s][1]))
            for s in range(2)
        ]

    h_copies = [
        side_copies(pl.ds(64 * (2 * a), 64 * (a + 1)), hs_sem.at[a], hr_sem.at[a]) for a in range(2)
    ]
    e_copies = [
        side_copies(pl.ds(64 * (3 * a + 1), 64 * (a + 1)), es_sem.at[a], er_sem.at[a])
        for a in range(2)
    ]

    def start(group):
        for sends, _, copy in group:
            @pl.when(sends)
            def _():
                copy.start()

    def arrive(group):
        for _, comes, copy in group:
            @pl.when(comes)
            def _():
                copy.wait_recv()

    def sent(group):
        for sends, _, copy in group:
            @pl.when(sends)
            def _():
                copy.wait_send()

    start(v_copies[0])
    start(h_copies[0])
    start(v_copies[1])
    start(v_copies[2])
    start(h_copies[1])

    for copy in const_copies:
        copy.wait()
    con = Consts(dict(zip(names, const_vmem)))
    left = con.one("left")
    own = con.one("own")
    for k in range(6):
        high, low = build_left(k, left, own)
        left_hi[64 * k : 64 * k + 64, :] = high
        left_lo[64 * k : 64 * k + 64, :] = low
    for part in range(2):
        table = con.one("left_t")[:, 128 * part : 128 * part + 128]
        for pair in range(3):
            mask = con.one("own_t")[:, 128 * pair : 128 * pair + 128]
            high, low = split(table * mask)
            where = 384 * part + 128 * pair
            left_t_hi[:, where : where + 128] = high
            left_t_lo[:, where : where + 128] = low

    for copy in x_copies:
        copy.wait_recv()
    for c in range(2):
        parts = [
            jnp.concatenate([x_buf[i, p, c : c + 1, :] for i in range(8)], axis=0)
            for p in range(4)
        ]
        y_send[c] = jnp.concatenate(parts + [jnp.zeros((8, 32), F32)], axis=1)
    mine = core * 8 + y
    y_copies = [
        remote(y_send, h_buf.at[mine], ys_sem.at[i], yr_sem.at[i], peer)
        for i, peer in enumerate(yc_peers)
    ]
    for copy in y_copies:
        copy.start()
    h_buf[mine] = y_send[...]

    arrive(v_copies[0])
    pack_logits(vert[0], 64)
    start(e_copies[0])
    arrive(v_copies[1])
    arrive(v_copies[2])
    pack_pair(vert[1], vert[2], 128)
    start(e_copies[1])

    arrive(h_copies[0])
    arrive(e_copies[0])
    fold_right = jnp.concatenate(unfolded(from_right[0:128]), axis=0)
    fold_left = jnp.concatenate(unfolded_high(from_left[0:128]), axis=0)
    logits = logits_ref[...]
    lane = lax.broadcasted_iota(jnp.int32, (256, 128), 1)
    wide = jnp.concatenate(
        [
            jnp.concatenate([logits, vert[0]], axis=0),
            jnp.where(lane < 64, fold_right, fold_left),
        ],
        axis=1,
    )
    spec = spectrum(jax.nn.sigmoid(wide), con)

    for copy in y_copies:
        copy.wait_recv()
    bank = spread_bank([h_buf[:, c].reshape(128, 128) for c in range(2)])
    fields = fields_of(spec, bank, con, (left_hi[...], left_lo[...]))
    intensity = intensity_of(fields, con)

    arrive(h_copies[1])
    arrive(e_copies[1])
    pair_right = from_right[128:384]
    pair_left = from_left[128:384]
    goal = jnp.concatenate(
        [
            jnp.concatenate([target_ref[...], vert[1]], axis=0),
            jnp.where(lane < 64, pair_right, pltpu.roll(pair_left, 64, 1)),
        ],
        axis=1,
    )
    weight = jnp.concatenate(
        [
            jnp.concatenate([weight_ref[...], vert[2]], axis=0),
            jnp.where(lane < 64, pltpu.roll(pair_right, 64, 1), pair_left),
        ],
        axis=1,
    )
    slopes, losses = [], 0.0
    for c in range(2):
        slope, loss = slope_of(intensity[c], goal, weight, DOSES[c])
        slopes.append(slope)
        losses = losses + loss
    grad = gradient_of(slopes, fields, bank, con, (left_t_hi[...], left_t_lo[...]))
    mask = jax.nn.sigmoid(logits)
    grad = grad * mask * (1.0 - mask)

    total = jnp.concatenate(
        [jnp.sum(grad * grad, axis=0, keepdims=True), jnp.sum(losses, axis=0, keepdims=True)],
        axis=0,
    )
    slot = 0
    r_copies = []
    for stage, peers in enumerate((xz_peers, yc_peers)):
        r_send[stage] = total
        copies = [
            remote(r_send.at[stage], r_buf.at[slot + i], rs_sem.at[slot + i], rr_sem.at[slot + i], peer)
            for i, peer in enumerate(peers)
        ]
        for copy in copies:
            copy.start()
        for copy in copies:
            copy.wait_recv()
        for i in range(len(peers)):
            total = total + r_buf[slot + i]
        slot += len(peers)
        r_copies += copies

    squares = jnp.sum(total[0:1, :], axis=1, keepdims=True)
    loss_ref[0, 0] = jnp.sum(total[1:2, :]) / CELLS
    norm = jnp.sqrt(squares / CELLS + EPSILON)
    out_ref[...] = logits - 0.5 * grad / norm

    for group in v_copies + h_copies + e_copies:
        sent(group)
    for copy in x_copies + y_copies + r_copies:
        copy.wait_send()


def shards(mask_logits, target, weight, kernels):
    names, arrays = const_arrays()
    count = len(names)
    vmem = pl.BlockSpec(memory_space=pltpu.VMEM)
    dma = pltpu.SemaphoreType.DMA
    scratch = [pltpu.VMEM(a.shape, a.dtype) for a in arrays] + [
        pltpu.VMEM((384, 768), BF16), pltpu.VMEM((384, 768), BF16),
        pltpu.VMEM((384, 768), BF16), pltpu.VMEM((384, 768), BF16),
        pltpu.VMEM((3, 128, 128), F32),
        pltpu.VMEM((2, 384, 128), F32), pltpu.VMEM((384, 128), F32), pltpu.VMEM((384, 128), F32),
        pltpu.VMEM((8, 4, 2, 24), F32),
        pltpu.VMEM((2, 8, 128), F32), pltpu.VMEM((16, 2, 8, 128), F32),
        pltpu.VMEM((2, 2, 128), F32), pltpu.VMEM((46, 2, 128), F32),
        dma((count,)), dma((3, 2)), dma((3, 2)), dma((2, 2)), dma((2, 2)), dma((2, 2)), dma((2, 2)),
        dma((31,)), dma((31,)), dma((15,)), dma((15,)), dma((46,)), dma((46,)),
    ]
    new_logits, loss = pl.pallas_call(
        functools.partial(kernel, names),
        out_shape=(
            jax.ShapeDtypeStruct((128, 128), F32),
            jax.ShapeDtypeStruct((1, 1), F32),
        ),
        in_specs=[vmem] * 4 + [pl.BlockSpec(memory_space=pl.ANY)] * count,
        out_specs=(vmem, pl.BlockSpec(memory_space=pltpu.SMEM)),
        scratch_shapes=scratch,
        compiler_params=pltpu.CompilerParams(collective_id=0, has_side_effects=True),
        name="litho",
    )(mask_logits, target, weight, kernels, *[jnp.asarray(a) for a in arrays])
    return new_logits, loss.reshape(())


def solution(mesh):
    placed = (P("row", "col"), P("row", "col"), P("row", "col"), P(None, ("row", "col")))
    return jax.shard_map(
        shards, mesh=mesh, in_specs=placed, out_specs=(P("row", "col"), P()), check_vma=False
    )
```

```python
import functools

import numpy as np
import ml_dtypes

import jax
import jax.numpy as jnp
from jax import lax
from jax.experimental import pallas as pl
from jax.experimental.pallas import tpu as pltpu
from jax.sharding import PartitionSpec as P

MESH = pl.DeviceIdType.MESH
F32 = jnp.float32
BF16 = jnp.bfloat16
DOSES = (1.0, 1.15)
EPSILON = 1e-06
CELLS = 4096 * 2048
GRID = 64
ROWS_H = 384


def tables():
    place = np.concatenate([np.arange(64, 192), np.arange(192, 256), np.arange(0, 64)])
    freq = np.arange(32) - 16

    def wave(points):
        turn = 2 * np.pi * ((freq[:, None] * points[None, :]) % 256) / 256
        return np.cos(turn) / 16, np.sin(turn) / 16

    cos_p, sin_p = wave(place)
    cos_g, sin_g = wave(4 * np.arange(GRID))
    out = {}
    mask_re = np.concatenate([cos_p.T, -sin_p.T], 1)
    mask_im = np.concatenate([sin_p.T, cos_p.T], 1)
    out["first"] = np.concatenate([mask_re, mask_re, mask_im, mask_im], 1)
    out["second"] = np.concatenate([cos_p, sin_p], 0)
    line, block = np.divmod(np.arange(ROWS_H), 128)
    core, y, part, low = block // 64, block // 8 % 8, block // 4 % 2, block % 4
    number = 3 * ((y * 2 + core) * 4 + low) + line
    kernel, u = number // 32, number % 32
    out["pick"] = (u[:, None] == np.arange(32)[None, :]).astype(np.float64)
    left_c = np.where(part[:, None] == 0, cos_g[u], -sin_g[u])
    left_d = np.where(part[:, None] == 0, sin_g[u], cos_g[u])
    out["left"] = np.concatenate([left_c, left_d], 0).T
    out["left_t"] = np.concatenate([left_c, left_c, left_d, left_d], 1)
    same = kernel[:, None] == np.arange(6)[None, :]
    out["own"] = np.concatenate([np.tile(same.T, (1, 2)), np.zeros((2, 768))], 0)
    out["own_t"] = np.repeat(same, 64, axis=1).astype(np.float64)
    zero = np.zeros((64, 128))
    right = np.concatenate(
        [np.concatenate([cos_g, sin_g], 1), np.concatenate([-sin_g, cos_g], 1)], 0
    )
    out["right"] = np.concatenate(
        [np.concatenate([right, zero], 1), np.concatenate([zero, right], 1)], 0
    )
    gap = place[:, None] - 4 * np.arange(GRID)[None, :]
    order = np.arange(1, 32)
    spread = (1 + 2 * np.cos(2 * np.pi * (gap[..., None] * order % 256) / 256).sum(-1)) / 64
    out["up_cols"] = np.concatenate([spread.T, spread.T], 0)
    out["up_rows"] = spread
    out["down_rows"] = spread.T
    out["down_cols"] = np.concatenate([spread, spread], 1)
    back = np.concatenate(
        [np.concatenate([cos_g.T, -sin_g.T], 1), np.concatenate([sin_g.T, cos_g.T], 1)], 0
    )
    turned = np.concatenate(
        [np.concatenate([-sin_g.T, -cos_g.T], 1), np.concatenate([cos_g.T, -sin_g.T], 1)], 0
    )
    zero = np.zeros((128, 64))
    out["back"] = np.concatenate(
        [
            np.concatenate([back, zero, turned, zero], 1),
            np.concatenate([zero, back, zero, turned], 1),
        ],
        0,
    )
    cos_c, sin_c = cos_p[:, :128], sin_p[:, :128]
    out["last_rows"] = np.concatenate([cos_c.T[:, u], sin_c.T[:, u]], 0)
    out["last_cols"] = 2 * np.concatenate(
        [cos_c, -sin_c, cos_c, -sin_c, -sin_c, -cos_c, -sin_c, -cos_c], 0
    )
    return out


SPLIT = (
    "first", "second", "right", "up_cols", "up_rows", "down_rows", "down_cols",
    "back", "last_rows", "last_cols",
)
PLAIN = ("left", "left_t", "own", "own_t")


def const_arrays():
    made = tables()
    names, arrays = [], []
    for name in SPLIT:
        value = made[name].astype(np.float32)
        high = value.astype(ml_dtypes.bfloat16)
        low = (value - high.astype(np.float32)).astype(ml_dtypes.bfloat16)
        names += [name + "_hi", name + "_lo"]
        arrays += [high, low]
    for name in PLAIN:
        names.append(name)
        arrays.append(made[name].astype(np.float32))
    names.append("pick")
    arrays.append(made["pick"].astype(ml_dtypes.bfloat16))
    return names, arrays


def split(value):
    high = value.astype(BF16)
    return high, (value - high.astype(F32)).astype(BF16)


def dot(first, second):
    return jnp.dot(first, second, preferred_element_type=F32)


def mm(first, second):
    return dot(first[0], second[0]) + (dot(first[1], second[0]) + dot(first[0], second[1]))


def build_left(k, left, own):
    return split(left * own[k : k + 1, :])


def spectrum(mask, con):
    half = mm(split(mask), con("first"))
    both = mm(con("second"), split(half))
    plain = both[:32, :128] - both[32:, 128:]
    turned = both[:32, 128:] + both[32:, :128]
    high, low = split(jnp.concatenate([plain, turned], axis=1))
    return dot(con.one("pick"), high) + dot(con.one("pick"), low)


def spread_bank(bank):
    lane = lax.broadcasted_iota(jnp.int32, (128, 128), 1)
    out = []
    for line in range(3):
        rolls = []
        for slot in range(4):
            shift = (32 * slot - 32 * line) % 128
            value = bank[slot // 2]
            rolls.append(value if shift == 0 else pltpu.roll(value, shift, 1))
        low = jnp.where(lane < 32, rolls[0], rolls[1])
        high = jnp.where(lane < 96, rolls[2], rolls[3])
        out.append(jnp.where(lane < 64, low, high))
    return jnp.concatenate(out, axis=0)


def fields_of(spec, bank, con, left):
    first = bank * spec[:, :128]
    second = bank * spec[:, 128:]
    lines = mm(left, split(jnp.concatenate([first, second], axis=0)))
    return mm(split(lines), con("right"))


def intensity_of(fields, con):
    square = fields * fields
    total = square[:64]
    for k in range(1, 6):
        total = total + square[64 * k : 64 * k + 64]
    stacked = jnp.concatenate([total[:, :128], total[:, 128:]], axis=0)
    wide = split(mm(split(stacked), con("up_cols")))
    return [mm(con("up_rows"), (wide[0][64 * c : 64 * c + 64], wide[1][64 * c : 64 * c + 64])) for c in range(2)]


def slope_of(intensity, target, weight, dose):
    resist = jax.nn.sigmoid(6.0 * (dose * intensity - 0.75))
    error = resist - target
    scaled = weight * error
    slope = (12.0 * dose) * scaled * resist * (1.0 - resist)
    return slope, (scaled * error)[:128, :128]


def gradient_of(slopes, fields, bank, con, left_t):
    rows = [mm(con("down_rows"), split(slope)) for slope in slopes]
    down = mm(split(jnp.concatenate(rows, axis=0)), con("down_cols"))
    pair = jnp.concatenate([down[:64], down[64:]], axis=1)
    moved = fields * jnp.concatenate([pair] * 6, axis=0)
    lines = mm(split(moved), con("back"))
    stacked = jnp.concatenate([lines[:, :128], lines[:, 128:]], axis=0)
    terms = bank * mm(left_t, split(stacked))
    last = mm(con("last_rows"), split(terms))
    return mm(split(jnp.concatenate([last[:128], last[128:]], axis=1)), con("last_cols"))


class Consts:
    def __init__(self, refs):
        self.refs = refs

    def __call__(self, name):
        return self.refs[name + "_hi"][...], self.refs[name + "_lo"][...]

    def one(self, name):
        return self.refs[name][...]


def kernel(names, *args):
    count = len(names)
    inputs_hbm = args[:4]
    const_hbm = args[4 : 4 + count]
    out_ref, loss_ref = args[4 + count : 6 + count]
    const_vmem = args[6 + count : 6 + 2 * count]
    (
        logits_ref, target_ref, weight_ref, bank_ref,
        left_hi, left_lo, left_t_hi, left_t_lo, vert, pack, from_left, from_right,
        x_buf, y_send, h_buf, r_send, r_buf,
        i_sem, c_sem, vs_sem, vr_sem, hs_sem, hr_sem, es_sem, er_sem,
        xs_sem, xr_sem, ys_sem, yr_sem, rs_sem, rr_sem,
    ) = args[6 + 2 * count :]

    row = lax.axis_index("row")
    col = lax.axis_index("col")
    core = row % 2
    y = row // 2 % 8
    z_hi = row // 16
    z_lo = col // 4
    x = col % 4
    z = z_hi * 4 + z_lo

    def at(z_, y_, core_, x_):
        return ((z_ // 4 * 8 + y_) * 2 + core_, z_ % 4 * 4 + x_)

    xz_peers = [at((z + d) % 8, y, core, (x + e) % 4) for d in range(8) for e in range(4) if d + e]
    yc_peers = [at(z, (y + d) % 8, (core + e) % 2, x) for d in range(8) for e in range(2) if d + e]
    sides = [
        (row > 0, (row - 1, col)),
        (row < 31, (row + 1, col)),
        (col > 0, (row, col - 1)),
        (col < 15, (row, col + 1)),
    ]

    barrier = pltpu.get_barrier_semaphore()
    for peer in xz_peers + yc_peers:
        pl.semaphore_signal(barrier, inc=1, device_id=peer, device_id_type=MESH)
    waits = 46
    for there, peer in sides:
        @pl.when(there)
        def _():
            pl.semaphore_signal(barrier, inc=1, device_id=peer, device_id_type=MESH)
        waits = waits + there.astype(jnp.int32)

    inputs = (logits_ref, target_ref, weight_ref, bank_ref)
    input_copies = [
        pltpu.make_async_copy(inputs_hbm[i], inputs[i], i_sem.at[i]) for i in range(4)
    ]
    for copy in input_copies:
        copy.start()
    const_copies = [
        pltpu.make_async_copy(const_hbm[i], const_vmem[i], c_sem.at[i]) for i in range(count)
    ]
    for copy in const_copies:
        copy.start()

    def fill_rows(first):
        vert[0, first : first + 64] = jnp.full((64, 128), -1000.0, F32)
        for a in (1, 2):
            vert[a, first : first + 64] = jnp.zeros((64, 128), F32)

    def fill_side(ref):
        ref[0:128] = jnp.full((128, 128), -1000.0, F32)
        ref[128:384] = jnp.zeros((256, 128), F32)

    for missing, fill, where in (
        (row == 0, fill_rows, 64),
        (row == 31, fill_rows, 0),
        (col == 0, fill_side, from_left),
        (col == 15, fill_side, from_right),
    ):
        @pl.when(missing)
        def _():
            fill(where)

    low_lanes = lax.broadcasted_iota(jnp.int32, (64, 128), 1) < 64
    low_pair = lax.broadcasted_iota(jnp.int32, (128, 128), 1) < 64

    def pack_logits(block, line):
        top, bottom = block[:64], block[64:]
        pack[0, line : line + 64] = jnp.where(low_lanes, top, pltpu.roll(bottom, 64, 1))
        pack[1, line : line + 64] = jnp.where(low_lanes, pltpu.roll(top, 64, 1), bottom)

    def unfolded(block):
        core_rows, margin = block[:64], block[64:]
        return [core_rows, pltpu.roll(core_rows, 64, 1), margin, pltpu.roll(margin, 64, 1)]

    def unfolded_high(block):
        core_rows, margin = block[:64], block[64:]
        return [pltpu.roll(core_rows, 64, 1), core_rows, pltpu.roll(margin, 64, 1), margin]

    def pack_pair(first, second, line):
        line = line + 128
        pack[0, line : line + 128] = jnp.where(low_pair, first, pltpu.roll(second, 64, 1))
        pack[1, line : line + 128] = jnp.where(low_pair, pltpu.roll(first, 64, 1), second)

    for copy in input_copies:
        copy.wait()
    pack_logits(logits_ref[...], 0)
    pack_pair(target_ref[...], weight_ref[...], 0)

    pl.semaphore_wait(barrier, waits)

    def remote(src, dst, send, recv, peer):
        return pltpu.make_async_remote_copy(
            src_ref=src, dst_ref=dst, send_sem=send, recv_sem=recv,
            device_id=peer, device_id_type=MESH,
        )

    x_copies = [
        remote(bank_ref, x_buf.at[z, x], xs_sem.at[i], xr_sem.at[i], peer)
        for i, peer in enumerate(xz_peers)
    ]
    for copy in x_copies:
        copy.start()
    x_buf[z, x] = bank_ref[...]

    sources = (logits_ref, target_ref, weight_ref)
    v_copies = [
        [
            (sides[s][0], sides[1 - s][0], remote(
                sources[a].at[pl.ds(64 * s, 64)], vert.at[a, pl.ds(64 * s, 64)],
                vs_sem.at[a, s], vr_sem.at[a, s], sides[s][1]))
            for s in range(2)
        ]
        for a in range(3)
    ]

    def side_copies(lines, send, recv):
        return [
            (sides[2 + s][0], sides[3 - s][0], remote(
                pack.at[s, lines], (from_right, from_left)[s].at[lines],
                send.at[s], recv.at[s], sides[2 + s][1]))
            for s in range(2)
        ]

    h_copies = [
        side_copies(pl.ds(64 * (2 * a), 64 * (a + 1)), hs_sem.at[a], hr_sem.at[a]) for a in range(2)
    ]
    e_copies = [
        side_copies(pl.ds(64 * (3 * a + 1), 64 * (a + 1)), es_sem.at[a], er_sem.at[a])
        for a in range(2)
    ]

    def start(group):
        for sends, _, copy in group:
            @pl.when(sends)
            def _():
                copy.start()

    def arrive(group):
        for _, comes, copy in group:
            @pl.when(comes)
            def _():
                copy.wait_recv()

    def sent(group):
        for sends, _, copy in group:
            @pl.when(sends)
            def _():
                copy.wait_send()

    start(v_copies[0])
    start(h_copies[0])
    start(v_copies[1])
    start(v_copies[2])
    start(h_copies[1])

    for copy in const_copies:
        copy.wait()
    con = Consts(dict(zip(names, const_vmem)))
    left = con.one("left")
    own = con.one("own")
    for k in range(6):
        high, low = build_left(k, left, own)
        left_hi[64 * k : 64 * k + 64, :] = high
        left_lo[64 * k : 64 * k + 64, :] = low
    for part in range(2):
        table = con.one("left_t")[:, 128 * part : 128 * part + 128]
        for pair in range(3):
            mask = con.one("own_t")[:, 128 * pair : 128 * pair + 128]
            high, low = split(table * mask)
            where = 384 * part + 128 * pair
            left_t_hi[:, where : where + 128] = high
            left_t_lo[:, where : where + 128] = low

    for copy in x_copies:
        copy.wait_recv()
    for c in range(2):
        parts = [
            jnp.concatenate([x_buf[i, p, c : c + 1, :] for i in range(8)], axis=0)
            for p in range(4)
        ]
        y_send[c] = jnp.concatenate(parts + [jnp.zeros((8, 32), F32)], axis=1)
    mine = core * 8 + y
    y_copies = [
        remote(y_send, h_buf.at[mine], ys_sem.at[i], yr_sem.at[i], peer)
        for i, peer in enumerate(yc_peers)
    ]
    for copy in y_copies:
        copy.start()
    h_buf[mine] = y_send[...]

    arrive(v_copies[0])
    pack_logits(vert[0], 64)
    start(e_copies[0])
    arrive(v_copies[1])
    arrive(v_copies[2])
    pack_pair(vert[1], vert[2], 128)
    start(e_copies[1])

    arrive(h_copies[0])
    arrive(e_copies[0])
    fold_right = jnp.concatenate(unfolded(from_right[0:128]), axis=0)
    fold_left = jnp.concatenate(unfolded_high(from_left[0:128]), axis=0)
    logits = logits_ref[...]
    lane = lax.broadcasted_iota(jnp.int32, (256, 128), 1)
    wide = jnp.concatenate(
        [
            jnp.concatenate([logits, vert[0]], axis=0),
            jnp.where(lane < 64, fold_right, fold_left),
        ],
        axis=1,
    )
    spec = spectrum(jax.nn.sigmoid(wide), con)

    for copy in y_copies:
        copy.wait_recv()
    bank = spread_bank([h_buf[:, c].reshape(128, 128) for c in range(2)])
    fields = fields_of(spec, bank, con, (left_hi[...], left_lo[...]))
    intensity = intensity_of(fields, con)

    arrive(h_copies[1])
    arrive(e_copies[1])
    pair_right = from_right[128:384]
    pair_left = from_left[128:384]
    goal = jnp.concatenate(
        [
            jnp.concatenate([target_ref[...], vert[1]], axis=0),
            jnp.where(lane < 64, pair_right, pltpu.roll(pair_left, 64, 1)),
        ],
        axis=1,
    )
    weight = jnp.concatenate(
        [
            jnp.concatenate([weight_ref[...], vert[2]], axis=0),
            jnp.where(lane < 64, pltpu.roll(pair_right, 64, 1), pair_left),
        ],
        axis=1,
    )
    slopes, losses = [], 0.0
    for c in range(2):
        slope, loss = slope_of(intensity[c], goal, weight, DOSES[c])
        slopes.append(slope)
        losses = losses + loss
    grad = gradient_of(slopes, fields, bank, con, (left_t_hi[...], left_t_lo[...]))
    mask = jax.nn.sigmoid(logits)
    grad = grad * mask * (1.0 - mask)

    total = jnp.concatenate(
        [jnp.sum(grad * grad, axis=0, keepdims=True), jnp.sum(losses, axis=0, keepdims=True)],
        axis=0,
    )
    slot = 0
    r_copies = []
    for stage, peers in enumerate((xz_peers, yc_peers)):
        r_send[stage] = total
        copies = [
            remote(r_send.at[stage], r_buf.at[slot + i], rs_sem.at[slot + i], rr_sem.at[slot + i], peer)
            for i, peer in enumerate(peers)
        ]
        for copy in copies:
            copy.start()
        for copy in copies:
            copy.wait_recv()
        for i in range(len(peers)):
            total = total + r_buf[slot + i]
        slot += len(peers)
        r_copies += copies

    squares = jnp.sum(total[0:1, :], axis=1, keepdims=True)
    loss = jnp.sum(total[1:2, :], axis=1, keepdims=True) / CELLS
    loss_ref[...] = jnp.broadcast_to(loss, (1, 128))
    norm = jnp.sqrt(squares / CELLS + EPSILON)
    out_ref[...] = logits - 0.5 * grad / norm

    for group in v_copies + h_copies + e_copies:
        sent(group)
    for copy in x_copies + y_copies + r_copies:
        copy.wait_send()


def shards(mask_logits, target, weight, kernels):
    names, arrays = const_arrays()
    count = len(names)
    vmem = pl.BlockSpec(memory_space=pltpu.VMEM)
    dma = pltpu.SemaphoreType.DMA
    scratch = [pltpu.VMEM(a.shape, a.dtype) for a in arrays] + [
        pltpu.VMEM((128, 128), F32), pltpu.VMEM((128, 128), F32), pltpu.VMEM((128, 128), F32),
        pltpu.VMEM((2, 24), F32),
        pltpu.VMEM((384, 768), BF16), pltpu.VMEM((384, 768), BF16),
        pltpu.VMEM((384, 768), BF16), pltpu.VMEM((384, 768), BF16),
        pltpu.VMEM((3, 128, 128), F32),
        pltpu.VMEM((2, 384, 128), F32), pltpu.VMEM((384, 128), F32), pltpu.VMEM((384, 128), F32),
        pltpu.VMEM((8, 4, 2, 24), F32),
        pltpu.VMEM((2, 8, 128), F32), pltpu.VMEM((16, 2, 8, 128), F32),
        pltpu.VMEM((2, 2, 128), F32), pltpu.VMEM((46, 2, 128), F32),
        dma((4,)), dma((count,)), dma((3, 2)), dma((3, 2)), dma((2, 2)), dma((2, 2)), dma((2, 2)), dma((2, 2)),
        dma((31,)), dma((31,)), dma((15,)), dma((15,)), dma((46,)), dma((46,)),
    ]
    new_logits, loss = pl.pallas_call(
        functools.partial(kernel, names),
        out_shape=(pltpu.VMEM((128, 128), F32), pltpu.VMEM((1, 128), F32)),
        in_specs=[pl.BlockSpec(memory_space=pl.ANY)] * (4 + count),
        out_specs=(vmem, vmem),
        scratch_shapes=scratch,
        compiler_params=pltpu.CompilerParams(collective_id=0, has_side_effects=True),
        name="litho",
    )(mask_logits, target, weight, kernels, *[jnp.asarray(a) for a in arrays])
    return new_logits, loss[0, 0]


def solution(mesh):
    placed = (P("row", "col"), P("row", "col"), P("row", "col"), P(None, ("row", "col")))
    return jax.shard_map(
        shards, mesh=mesh, in_specs=placed, out_specs=(P("row", "col"), P()), check_vma=False
    )
```

```python
import functools

import numpy as np
import ml_dtypes

import jax
import jax.numpy as jnp
from jax import lax
from jax.experimental import pallas as pl
from jax.experimental.pallas import tpu as pltpu
from jax.sharding import PartitionSpec as P

MESH = pl.DeviceIdType.MESH
F32 = jnp.float32
BF16 = jnp.bfloat16
DOSES = (1.0, 1.15)
EPSILON = 1e-06
CELLS = 4096 * 2048
GRID = 64
ROWS_H = 384


def tables():
    place = np.concatenate([np.arange(64, 192), np.arange(192, 256), np.arange(0, 64)])
    freq = np.arange(32) - 16

    def wave(points):
        turn = 2 * np.pi * ((freq[:, None] * points[None, :]) % 256) / 256
        return np.cos(turn) / 16, np.sin(turn) / 16

    cos_p, sin_p = wave(place)
    cos_g, sin_g = wave(4 * np.arange(GRID))
    out = {}
    mask_re = np.concatenate([cos_p.T, -sin_p.T], 1)
    mask_im = np.concatenate([sin_p.T, cos_p.T], 1)
    out["first"] = np.concatenate([mask_re, mask_re, mask_im, mask_im], 1)
    out["second"] = np.concatenate([cos_p, sin_p], 0)
    line, block = np.divmod(np.arange(ROWS_H), 128)
    core, y, part, low = block // 64, block // 8 % 8, block // 4 % 2, block % 4
    number = 3 * ((y * 2 + core) * 4 + low) + line
    kernel, u = number // 32, number % 32
    out["pick"] = (u[:, None] == np.arange(32)[None, :]).astype(np.float64)
    left_c = np.where(part[:, None] == 0, cos_g[u], -sin_g[u])
    left_d = np.where(part[:, None] == 0, sin_g[u], cos_g[u])
    out["left"] = np.concatenate([left_c, left_d], 0).T
    out["left_t"] = np.concatenate([left_c, left_c, left_d, left_d], 1)
    same = kernel[:, None] == np.arange(6)[None, :]
    out["own"] = np.concatenate([np.tile(same.T, (1, 2)), np.zeros((2, 768))], 0)
    out["own_t"] = np.repeat(same, 64, axis=1).astype(np.float64)
    zero = np.zeros((64, 128))
    right = np.concatenate(
        [np.concatenate([cos_g, sin_g], 1), np.concatenate([-sin_g, cos_g], 1)], 0
    )
    out["right"] = np.concatenate(
        [np.concatenate([right, zero], 1), np.concatenate([zero, right], 1)], 0
    )
    gap = place[:, None] - 4 * np.arange(GRID)[None, :]
    order = np.arange(1, 32)
    spread = (1 + 2 * np.cos(2 * np.pi * (gap[..., None] * order % 256) / 256).sum(-1)) / 64
    out["up_cols"] = np.concatenate([spread.T, spread.T], 0)
    out["up_rows"] = spread
    out["down_rows"] = spread.T
    out["down_cols"] = np.concatenate([spread, spread], 1)
    back = np.concatenate(
        [np.concatenate([cos_g.T, -sin_g.T], 1), np.concatenate([sin_g.T, cos_g.T], 1)], 0
    )
    turned = np.concatenate(
        [np.concatenate([-sin_g.T, -cos_g.T], 1), np.concatenate([cos_g.T, -sin_g.T], 1)], 0
    )
    zero = np.zeros((128, 64))
    out["back"] = np.concatenate(
        [
            np.concatenate([back, zero, turned, zero], 1),
            np.concatenate([zero, back, zero, turned], 1),
        ],
        0,
    )
    cos_c, sin_c = cos_p[:, :128], sin_p[:, :128]
    out["last_rows"] = np.concatenate([cos_c.T[:, u], sin_c.T[:, u]], 0)
    out["last_cols"] = 2 * np.concatenate(
        [cos_c, -sin_c, cos_c, -sin_c, -sin_c, -cos_c, -sin_c, -cos_c], 0
    )
    return out


SPLIT = (
    "first", "second", "right", "up_cols", "up_rows", "down_rows", "down_cols",
    "back", "last_rows", "last_cols",
)
PLAIN = ("left", "left_t", "own", "own_t")


def const_arrays():
    made = tables()
    names, arrays = [], []
    for name in SPLIT:
        value = made[name].astype(np.float32)
        high = value.astype(ml_dtypes.bfloat16)
        low = (value - high.astype(np.float32)).astype(ml_dtypes.bfloat16)
        names += [name + "_hi", name + "_lo"]
        arrays += [high, low]
    for name in PLAIN:
        names.append(name)
        arrays.append(made[name].astype(np.float32))
    names.append("pick")
    arrays.append(made["pick"].astype(ml_dtypes.bfloat16))
    return names, arrays


def split(value):
    high = value.astype(BF16)
    return high, (value - high.astype(F32)).astype(BF16)


def dot(first, second):
    return jnp.dot(first, second, preferred_element_type=F32)


def mm(first, second):
    if first[0].shape[1] % 128:
        return dot(first[0], second[0]) + (dot(first[1], second[0]) + dot(first[0], second[1]))
    return dot(
        jnp.concatenate([first[0], first[1], first[0]], axis=1),
        jnp.concatenate([second[0], second[0], second[1]], axis=0),
    )


def build_left(k, left, own):
    return split(left * own[k : k + 1, :])


def spectrum(mask, con):
    half = mm(split(mask), con("first"))
    both = mm(con("second"), split(half))
    plain = both[:32, :128] - both[32:, 128:]
    turned = both[:32, 128:] + both[32:, :128]
    high, low = split(jnp.concatenate([plain, turned], axis=1))
    return dot(con.one("pick"), high) + dot(con.one("pick"), low)


def spread_bank(bank):
    lane = lax.broadcasted_iota(jnp.int32, (128, 128), 1)
    out = []
    for line in range(3):
        rolls = []
        for slot in range(4):
            shift = (32 * slot - 32 * line) % 128
            value = bank[slot // 2]
            rolls.append(value if shift == 0 else pltpu.roll(value, shift, 1))
        low = jnp.where(lane < 32, rolls[0], rolls[1])
        high = jnp.where(lane < 96, rolls[2], rolls[3])
        out.append(jnp.where(lane < 64, low, high))
    return jnp.concatenate(out, axis=0)


def fields_of(spec, bank, con, left):
    first = bank * spec[:, :128]
    second = bank * spec[:, 128:]
    lines = mm(left, split(jnp.concatenate([first, second], axis=0)))
    return mm(split(lines), con("right"))


def intensity_of(fields, con):
    square = fields * fields
    total = square[:64]
    for k in range(1, 6):
        total = total + square[64 * k : 64 * k + 64]
    stacked = jnp.concatenate([total[:, :128], total[:, 128:]], axis=0)
    wide = split(mm(split(stacked), con("up_cols")))
    return [mm(con("up_rows"), (wide[0][64 * c : 64 * c + 64], wide[1][64 * c : 64 * c + 64])) for c in range(2)]


def slope_of(intensity, target, weight, dose):
    resist = jax.nn.sigmoid(6.0 * (dose * intensity - 0.75))
    error = resist - target
    scaled = weight * error
    slope = (12.0 * dose) * scaled * resist * (1.0 - resist)
    return slope, (scaled * error)[:128, :128]


def gradient_of(slopes, fields, bank, con, left_t):
    rows = [mm(con("down_rows"), split(slope)) for slope in slopes]
    down = mm(split(jnp.concatenate(rows, axis=0)), con("down_cols"))
    pair = jnp.concatenate([down[:64], down[64:]], axis=1)
    moved = fields * jnp.concatenate([pair] * 6, axis=0)
    lines = mm(split(moved), con("back"))
    stacked = jnp.concatenate([lines[:, :128], lines[:, 128:]], axis=0)
    terms = bank * mm(left_t, split(stacked))
    last = mm(con("last_rows"), split(terms))
    return mm(split(jnp.concatenate([last[:128], last[128:]], axis=1)), con("last_cols"))


class Consts:
    def __init__(self, refs):
        self.refs = refs

    def __call__(self, name):
        return self.refs[name + "_hi"][...], self.refs[name + "_lo"][...]

    def one(self, name):
        return self.refs[name][...]


def kernel(names, *args):
    count = len(names)
    inputs_hbm = args[:4]
    const_hbm = args[4 : 4 + count]
    out_ref, loss_ref = args[4 + count : 6 + count]
    const_vmem = args[6 + count : 6 + 2 * count]
    (
        logits_ref, target_ref, weight_ref, bank_ref,
        left_hi, left_lo, left_t_hi, left_t_lo, vert, pack, from_left, from_right,
        x_buf, x_all, y_send, h_buf, r_send, r_buf,
        i_sem, c_sem, vs_sem, vr_sem, hs_sem, hr_sem, es_sem, er_sem,
        xs_sem, xr_sem, ys_sem, yr_sem, rs_sem, rr_sem,
    ) = args[6 + 2 * count :]

    row = lax.axis_index("row")
    col = lax.axis_index("col")
    core = row % 2
    y = row // 2 % 8
    z_hi = row // 16
    z_lo = col // 4
    x = col % 4
    z = z_hi * 4 + z_lo

    def at(z_, y_, core_, x_):
        return ((z_ // 4 * 8 + y_) * 2 + core_, z_ % 4 * 4 + x_)

    def hops(d, n):
        return min(d, n - d)

    xz_steps = [(d, e) for d in range(8) for e in range(4) if d + e]
    xz_steps.sort(key=lambda s: (-hops(s[0], 8) - hops(s[1], 4), s))
    xz_peers = [at((z + d) % 8, y, core, (x + e) % 4) for d, e in xz_steps]
    yc_steps = [(d, e) for d in range(8) for e in range(2) if d + e]
    yc_steps.sort(key=lambda s: (-hops(s[0], 8), s))
    yc_peers = [at(z, (y + d) % 8, (core + e) % 2, x) for d, e in yc_steps]
    sides = [
        (row > 0, (row - 1, col)),
        (row < 31, (row + 1, col)),
        (col > 0, (row, col - 1)),
        (col < 15, (row, col + 1)),
    ]

    barrier = pltpu.get_barrier_semaphore()
    for peer in xz_peers + yc_peers:
        pl.semaphore_signal(barrier, inc=1, device_id=peer, device_id_type=MESH)
    waits = 46
    for there, peer in sides:
        @pl.when(there)
        def _():
            pl.semaphore_signal(barrier, inc=1, device_id=peer, device_id_type=MESH)
        waits = waits + there.astype(jnp.int32)

    inputs = (logits_ref, target_ref, weight_ref, bank_ref)
    input_copies = [
        pltpu.make_async_copy(inputs_hbm[i], inputs[i], i_sem.at[i]) for i in range(4)
    ]
    for copy in input_copies:
        copy.start()
    const_copies = [
        pltpu.make_async_copy(const_hbm[i], const_vmem[i], c_sem.at[i]) for i in range(count)
    ]
    for copy in const_copies:
        copy.start()

    def fill_rows(first):
        vert[0, first : first + 64] = jnp.full((64, 128), -1000.0, F32)
        for a in (1, 2):
            vert[a, first : first + 64] = jnp.zeros((64, 128), F32)

    def fill_side(ref):
        ref[0:128] = jnp.full((128, 128), -1000.0, F32)
        ref[128:384] = jnp.zeros((256, 128), F32)

    for missing, fill, where in (
        (row == 0, fill_rows, 64),
        (row == 31, fill_rows, 0),
        (col == 0, fill_side, from_left),
        (col == 15, fill_side, from_right),
    ):
        @pl.when(missing)
        def _():
            fill(where)

    low_lanes = lax.broadcasted_iota(jnp.int32, (64, 128), 1) < 64
    low_pair = lax.broadcasted_iota(jnp.int32, (128, 128), 1) < 64

    def pack_logits(block, line):
        top, bottom = block[:64], block[64:]
        pack[0, line : line + 64] = jnp.where(low_lanes, top, pltpu.roll(bottom, 64, 1))
        pack[1, line : line + 64] = jnp.where(low_lanes, pltpu.roll(top, 64, 1), bottom)

    def unfolded(block):
        core_rows, margin = block[:64], block[64:]
        return [core_rows, pltpu.roll(core_rows, 64, 1), margin, pltpu.roll(margin, 64, 1)]

    def unfolded_high(block):
        core_rows, margin = block[:64], block[64:]
        return [pltpu.roll(core_rows, 64, 1), core_rows, pltpu.roll(margin, 64, 1), margin]

    def pack_pair(first, second, line):
        line = line + 128
        pack[0, line : line + 128] = jnp.where(low_pair, first, pltpu.roll(second, 64, 1))
        pack[1, line : line + 128] = jnp.where(low_pair, pltpu.roll(first, 64, 1), second)

    for copy in input_copies:
        copy.wait()
    pack_logits(logits_ref[...], 0)
    pack_pair(target_ref[...], weight_ref[...], 0)

    pl.semaphore_wait(barrier, waits)

    def remote(src, dst, send, recv, peer):
        return pltpu.make_async_remote_copy(
            src_ref=src, dst_ref=dst, send_sem=send, recv_sem=recv,
            device_id=peer, device_id_type=MESH,
        )

    def drain(ref, sem):
        pltpu.make_async_copy(ref, ref, sem).wait()

    x_copies = [
        remote(bank_ref, x_buf.at[z, x], xs_sem, xr_sem, peer) for peer in xz_peers
    ]
    for copy in x_copies:
        copy.start()
    x_buf[z, x] = bank_ref[...]

    sources = (logits_ref, target_ref, weight_ref)
    v_copies = [
        [
            (sides[s][0], sides[1 - s][0], remote(
                sources[a].at[pl.ds(64 * s, 64)], vert.at[a, pl.ds(64 * s, 64)],
                vs_sem.at[a, s], vr_sem.at[a, s], sides[s][1]))
            for s in range(2)
        ]
        for a in range(3)
    ]

    def side_copies(lines, send, recv):
        return [
            (sides[2 + s][0], sides[3 - s][0], remote(
                pack.at[s, lines], (from_right, from_left)[s].at[lines],
                send.at[s], recv.at[s], sides[2 + s][1]))
            for s in range(2)
        ]

    h_copies = [
        side_copies(pl.ds(64 * (2 * a), 64 * (a + 1)), hs_sem.at[a], hr_sem.at[a]) for a in range(2)
    ]
    e_copies = [
        side_copies(pl.ds(64 * (3 * a + 1), 64 * (a + 1)), es_sem.at[a], er_sem.at[a])
        for a in range(2)
    ]

    def start(group):
        for sends, _, copy in group:
            @pl.when(sends)
            def _():
                copy.start()

    def arrive(group):
        for _, comes, copy in group:
            @pl.when(comes)
            def _():
                copy.wait_recv()

    def sent(group):
        for sends, _, copy in group:
            @pl.when(sends)
            def _():
                copy.wait_send()

    start(v_copies[0])
    start(h_copies[0])
    start(v_copies[1])
    start(v_copies[2])
    start(h_copies[1])

    for copy in const_copies:
        copy.wait()
    con = Consts(dict(zip(names, const_vmem)))
    left = con.one("left")
    own = con.one("own")
    for k in range(6):
        high, low = build_left(k, left, own)
        left_hi[64 * k : 64 * k + 64, :] = high
        left_lo[64 * k : 64 * k + 64, :] = low
    for part in range(2):
        table = con.one("left_t")[:, 128 * part : 128 * part + 128]
        for pair in range(3):
            mask = con.one("own_t")[:, 128 * pair : 128 * pair + 128]
            high, low = split(table * mask)
            where = 384 * part + 128 * pair
            left_t_hi[:, where : where + 128] = high
            left_t_lo[:, where : where + 128] = low

    drain(x_all, xr_sem)
    for c in range(2):
        parts = [
            jnp.concatenate([x_buf[i, p, c : c + 1, :] for i in range(8)], axis=0)
            for p in range(4)
        ]
        y_send[c] = jnp.concatenate(parts + [jnp.zeros((8, 32), F32)], axis=1)
    mine = core * 8 + y
    y_copies = [
        remote(y_send, h_buf.at[mine], ys_sem, yr_sem, peer) for peer in yc_peers
    ]
    for copy in y_copies:
        copy.start()
    h_buf[mine] = y_send[...]
    drain(x_all, xs_sem)

    arrive(v_copies[0])
    pack_logits(vert[0], 64)
    start(e_copies[0])
    arrive(v_copies[1])
    arrive(v_copies[2])
    pack_pair(vert[1], vert[2], 128)
    start(e_copies[1])

    arrive(h_copies[0])
    arrive(e_copies[0])
    fold_right = jnp.concatenate(unfolded(from_right[0:128]), axis=0)
    fold_left = jnp.concatenate(unfolded_high(from_left[0:128]), axis=0)
    logits = logits_ref[...]
    lane = lax.broadcasted_iota(jnp.int32, (256, 128), 1)
    wide = jnp.concatenate(
        [
            jnp.concatenate([logits, vert[0]], axis=0),
            jnp.where(lane < 64, fold_right, fold_left),
        ],
        axis=1,
    )
    spec = spectrum(jax.nn.sigmoid(wide), con)

    drain(h_buf.at[pl.ds(0, 15)], yr_sem)
    bank = spread_bank([h_buf[:, c].reshape(128, 128) for c in range(2)])
    fields = fields_of(spec, bank, con, (left_hi[...], left_lo[...]))
    intensity = intensity_of(fields, con)

    arrive(h_copies[1])
    arrive(e_copies[1])
    pair_right = from_right[128:384]
    pair_left = from_left[128:384]
    goal = jnp.concatenate(
        [
            jnp.concatenate([target_ref[...], vert[1]], axis=0),
            jnp.where(lane < 64, pair_right, pltpu.roll(pair_left, 64, 1)),
        ],
        axis=1,
    )
    weight = jnp.concatenate(
        [
            jnp.concatenate([weight_ref[...], vert[2]], axis=0),
            jnp.where(lane < 64, pltpu.roll(pair_right, 64, 1), pair_left),
        ],
        axis=1,
    )
    slopes, losses = [], 0.0
    for c in range(2):
        slope, loss = slope_of(intensity[c], goal, weight, DOSES[c])
        slopes.append(slope)
        losses = losses + loss
    grad = gradient_of(slopes, fields, bank, con, (left_t_hi[...], left_t_lo[...]))
    mask = jax.nn.sigmoid(logits)
    grad = grad * mask * (1.0 - mask)

    total = jnp.concatenate(
        [jnp.sum(grad * grad, axis=0, keepdims=True), jnp.sum(losses, axis=0, keepdims=True)],
        axis=0,
    )
    slot = 0
    stages = (xz_peers, yc_peers)
    blocks = [r_buf.at[pl.ds(0, 31)], r_buf.at[pl.ds(31, 15)]]
    for stage, peers in enumerate(stages):
        r_send[stage] = total
        for i, peer in enumerate(peers):
            remote(
                r_send.at[stage], r_buf.at[slot + i], rs_sem.at[stage], rr_sem.at[stage], peer
            ).start()
        if stage == 0:
            for group in v_copies + h_copies + e_copies:
                sent(group)
            drain(h_buf.at[pl.ds(0, 15)], ys_sem)
        else:
            drain(blocks[0], rs_sem.at[0])
        drain(blocks[stage], rr_sem.at[stage])
        total = total + jnp.sum(r_buf[slot : slot + len(peers)], axis=0)
        slot += len(peers)

    squares = jnp.sum(total[0:1, :], axis=1, keepdims=True)
    loss = jnp.sum(total[1:2, :], axis=1, keepdims=True) / CELLS
    loss_ref[...] = jnp.broadcast_to(loss, (1, 128))
    norm = jnp.sqrt(squares / CELLS + EPSILON)
    out_ref[...] = logits - 0.5 * grad / norm

    drain(blocks[1], rs_sem.at[1])


def shards(mask_logits, target, weight, kernels):
    names, arrays = const_arrays()
    count = len(names)
    vmem = pl.BlockSpec(memory_space=pltpu.VMEM)
    dma = pltpu.SemaphoreType.DMA
    scratch = [pltpu.VMEM(a.shape, a.dtype) for a in arrays] + [
        pltpu.VMEM((128, 128), F32), pltpu.VMEM((128, 128), F32), pltpu.VMEM((128, 128), F32),
        pltpu.VMEM((2, 24), F32),
        pltpu.VMEM((384, 768), BF16), pltpu.VMEM((384, 768), BF16),
        pltpu.VMEM((384, 768), BF16), pltpu.VMEM((384, 768), BF16),
        pltpu.VMEM((3, 128, 128), F32),
        pltpu.VMEM((2, 384, 128), F32), pltpu.VMEM((384, 128), F32), pltpu.VMEM((384, 128), F32),
        pltpu.VMEM((8, 4, 2, 24), F32), pltpu.VMEM((31, 2, 24), F32),
        pltpu.VMEM((2, 8, 128), F32), pltpu.VMEM((16, 2, 8, 128), F32),
        pltpu.VMEM((2, 2, 128), F32), pltpu.VMEM((46, 2, 128), F32),
        dma((4,)), dma((count,)), dma((3, 2)), dma((3, 2)), dma((2, 2)), dma((2, 2)), dma((2, 2)), dma((2, 2)),
        dma(()), dma(()), dma(()), dma(()), dma((2,)), dma((2,)),
    ]
    new_logits, loss = pl.pallas_call(
        functools.partial(kernel, names),
        out_shape=(pltpu.VMEM((128, 128), F32), pltpu.VMEM((1, 128), F32)),
        in_specs=[pl.BlockSpec(memory_space=pl.ANY)] * (4 + count),
        out_specs=(vmem, vmem),
        scratch_shapes=scratch,
        compiler_params=pltpu.CompilerParams(collective_id=0, has_side_effects=True),
        name="litho",
    )(mask_logits, target, weight, kernels, *[jnp.asarray(a) for a in arrays])
    return new_logits, loss[0, 0]


def solution(mesh):
    placed = (P("row", "col"), P("row", "col"), P("row", "col"), P(None, ("row", "col")))
    return jax.shard_map(
        shards, mesh=mesh, in_specs=placed, out_specs=(P("row", "col"), P()), check_vma=False
    )
```
